128 devices in a mesh: seq: 16 (over x, y_hi, core), tp: 8 (over z, y_lo).
Axes of the slice: x: 4, y: 4 (y_hi: 2, y_lo: 2; y = y_hi * 2 + y_lo), z: 4, core: 2. Of those that a mesh axis runs over, the one named last changes fastest.
Arguments:
- byte_ids: int32 [4096, 8], P('seq'), may hold values from 0 to 255
- global_out: bfloat16 [4096, 8192], P('seq', 'tp'), may hold values from -6 to 6
- global_in_grad: bfloat16 [4096, 8192], P('seq', 'tp'), may hold values from -6 to 6
- out_grad: bfloat16 [32768, 1024], P(('seq', 'tp')), may hold values from -6 to 6
- proj_weight: bfloat16 [1024, 1024], replicated, may hold values from -0.1875 to 0.1875
- emb_local: bfloat16 [256, 1024], replicated, may hold values from -6 to 6
- norm_gain: float32 [1024], replicated, may hold values from 0.1 to 1.9
- up_weight: bfloat16 [1024, 2048], replicated, may hold values from -0.1875 to 0.1875
- down_weight: bfloat16 [2048, 1024], replicated, may hold values from -0.125 to 0.125
Outputs:
- glob_out_grad: bfloat16 [4096, 8192], P('seq', 'tp')
- emb_global_grad: float32 [256, 1024], replicated
- emb_local_grad: float32 [256, 1024], replicated
- gain_grad: float32 [1024], replicated
- proj_grad: float32 [1024, 1024], P(None, ('seq', 'tp'))
- up_grad: float32 [1024, 2048], P(None, ('seq', 'tp'))
- down_grad: float32 [2048, 1024], P(('seq', 'tp'))
The draws below stay inside these ranges and needn't reach their ends.
All inputs are finite; a program needn't handle non-finite values.
Results may differ from the reference program's by a relative error of at most 0.015.
Values may be sent and summed in bfloat16 or wider, within the bound.
A program may use at most 128 MiB of HBM per device.

```python
import jax
import jax.numpy as jnp
from jax import lax

PATCH = 8
SLOT = 1024
DL = 1024
FF = 2048
VOCAB = 256
GW = 8192
PATCHES = 4096
BYTES = 32768


def with_ends(values, stream_key, smallest, largest):
    shape = values.shape
    index_at = [jax.random.randint(jax.random.fold_in(stream_key, axis), (), 0, shape[axis]) for axis in range(len(shape))]
    values = values.at[tuple(index_at)].set(smallest)
    longest = shape.index(max(shape))
    index_at[longest] = (index_at[longest] + 1) % shape[longest]
    return values.at[tuple(index_at)].set(largest)


def level_of(key, dims, split, low, top_value):
    def one(dim, shards_of):
        draws = jax.random.uniform(jax.random.fold_in(jax.random.fold_in(key, 6), dim), (shards_of,), jnp.float32, low / len(split), top_value / len(split))
        return jnp.repeat(jnp.exp(draws), dims[dim] // shards_of).reshape((-1,) + (1,) * (len(dims) - dim - 1))

    factor_of = one(*split[0])
    for cut in split[1:]:
        factor_of = factor_of * one(*cut)
    return factor_of


def scatter_about(own_key, extent, deviation, limit, split=(), kind=jnp.bfloat16):
    loudness = level_of(own_key, extent, split, -0.22, 0.18) if split else 1.0
    result = jax.random.normal(own_key, extent, jnp.float32) * deviation * loudness
    return jnp.minimum(jnp.maximum(result, -limit), limit).astype(kind)


def setup_inputs(seed: int = 0) -> dict:
    splits = jax.random.split(jax.random.key(seed), 10)
    byte_ids = with_ends(jax.random.randint(splits[0], (PATCHES, PATCH), 0, 256), jax.random.fold_in(splits[0], 1), 0, 255).astype(jnp.int32)
    global_out = scatter_about(splits[1], (PATCHES, GW), 1.0, 6.0, ((0, 16), (1, 8)))
    global_in_grad = scatter_about(splits[2], (PATCHES, GW), 1.0, 6.0, ((0, 16), (1, 8)))
    out_grad = scatter_about(splits[3], (BYTES, DL), 1.0, 6.0, ((0, 128),))
    proj_weight = scatter_about(splits[4], (SLOT, DL), SLOT ** -0.5, 0.1875)
    emb_local = scatter_about(splits[5], (VOCAB, DL), 1.0, 6.0)
    norm_gain = jnp.clip(1.0 + 0.18 * jax.random.normal(splits[6], (DL,), jnp.float32), 0.1, 1.9)
    up_weight = scatter_about(splits[7], (DL, FF), DL ** -0.5, 0.1875)
    down_weight = scatter_about(splits[8], (FF, DL), FF ** -0.5, 0.125)
    return {"byte_ids": byte_ids, "global_out": global_out, "global_in_grad": global_in_grad, "out_grad": out_grad, "proj_weight": proj_weight, "emb_local": emb_local, "norm_gain": norm_gain, "up_weight": up_weight, "down_weight": down_weight}


def inner(left, right):
    return lax.dot_general(left, right, (((0,), (0,)), ((), ())), preferred_element_type=jnp.float32)

def outer(left, right):
    return lax.dot_general(left, right, (((1,), (1,)), ((), ())), preferred_element_type=jnp.float32)

def reference(byte_ids, global_out, global_in_grad, out_grad, proj_weight, emb_local, norm_gain, up_weight, down_weight):
    slot_in = global_out.reshape(BYTES, SLOT)
    first = jnp.full((PATCHES, 1), -1, jnp.int32)
    prev_id = jnp.concatenate([first, byte_ids[:, :-1]], axis=1).reshape(BYTES)
    prev_hot = jax.nn.one_hot(prev_id, VOCAB, dtype=jnp.bfloat16)
    u_rows = jnp.dot(slot_in, proj_weight, preferred_element_type=jnp.float32) + jnp.dot(prev_hot, emb_local, preferred_element_type=jnp.float32)
    scale = lax.rsqrt(lax.optimization_barrier(jnp.mean(u_rows * u_rows, axis=1, keepdims=True)) + 1e-05)
    normed = u_rows * scale
    r_rows = (normed * norm_gain).astype(jnp.bfloat16)
    a_rows = jnp.dot(r_rows, up_weight, preferred_element_type=jnp.float32)
    sig = jax.nn.sigmoid(a_rows)
    h_rows = (a_rows * sig).astype(jnp.bfloat16)
    dh_rows = outer(out_grad, down_weight)
    da_rows = (dh_rows * sig * (1.0 + a_rows * (1.0 - sig))).astype(jnp.bfloat16)
    down_grad = inner(h_rows, out_grad)
    up_grad = inner(r_rows, da_rows)
    dr_rows = outer(da_rows, up_weight)
    gain_grad = lax.optimization_barrier(jnp.sum(dr_rows * normed, axis=0))
    dn_rows = dr_rows * norm_gain
    du_rows = (out_grad.astype(jnp.float32) + scale * (dn_rows - normed * lax.optimization_barrier(jnp.mean(dn_rows * normed, axis=1, keepdims=True)))).astype(jnp.bfloat16)
    proj_grad = inner(slot_in, du_rows)
    emb_local_grad = inner(prev_hot, du_rows)
    glob_out_grad = outer(du_rows, proj_weight).astype(jnp.bfloat16).reshape(PATCHES, GW)
    own_hot = jax.nn.one_hot(byte_ids.reshape(BYTES), VOCAB, dtype=jnp.bfloat16)
    emb_global_grad = inner(own_hot, global_in_grad.reshape(BYTES, SLOT))
    return (glob_out_grad, emb_global_grad, emb_local_grad, gain_grad, proj_grad, up_grad, down_grad)
```

```python
import functools

import jax
import jax.numpy as jnp
from jax import lax
from jax.experimental import pallas as pl
from jax.experimental.pallas import tpu as pltpu
from jax.sharding import PartitionSpec as P

BF = jnp.bfloat16
F32 = jnp.float32
MESH = pl.DeviceIdType.MESH
ALL = slice(None)
D_UNITS = ((0, 384, (0, 1, 2)), (384, 384, (1, 2, 0)), (768, 256, (2, 0, 1)))
M_UNITS = ((512, 256, (0, 1, 2)), (0, 256, (1, 2, 0)), (256, 256, (2, 0, 1)))
U_UNITS = ((0, 256, (0, 1, 2)), (256, 384, (1, 2, 0)), (640, 384, (2, 0, 1)))
ALL_UNITS = D_UNITS + M_UNITS + U_UNITS
M_WIDTH = 768


def mm(a, b):
    return lax.dot_general(a, b, (((1,), (0,)), ((), ())), preferred_element_type=F32)


def mm_nt(a, b):
    return lax.dot_general(a, b, (((1,), (1,)), ((), ())), preferred_element_type=F32)


def mm_tn(a, b):
    return lax.dot_general(a, b, (((0,), (0,)), ((), ())), preferred_element_type=F32)


def iota(shape, dim):
    return lax.broadcasted_iota(jnp.int32, shape, dim)


def remote(src, dst, send, recv, device):
    return pltpu.make_async_remote_copy(
        src_ref=src, dst_ref=dst, send_sem=send, recv_sem=recv, device_id=device, device_id_type=MESH
    )


class Ring:
    def __init__(self, src, axes, cols, over, half, spot, device_at, bufs, out, send, recv, base):
        self.src, self.axes, self.cols, self.over, self.half = src, axes, cols, over, half
        self.bufs, self.out, self.spot = bufs, out, spot
        here = spot[over]
        self.here, self.right, self.left, self.far = here, (here + 1) % 4, (here + 3) % 4, (here + 2) % 4
        self.to_right = device_at(over, self.right)
        self.to_left = device_at(over, self.left)
        self.sems = [(send.at[base + i], recv.at[base + i]) for i in range(6)]

    def part(self, place, half):
        index = tuple(
            place if a == self.over else pl.ds(2 * half, 2) if a == self.half else ALL for a in self.axes
        )
        cols = ALL if self.cols is None else pl.ds(*self.cols)
        return self.src.at[index + (ALL, cols)]

    def start(self):
        rel_a, rel_b, dir_a, dir_b, fin_a, fin_b = self.bufs
        s = self.sems
        self.c1 = remote(self.part(self.far, 0), rel_a, *s[0], self.to_right)
        self.d1 = remote(self.part(self.far, 1), rel_b, *s[1], self.to_left)
        self.c2 = remote(self.part(self.right, 1), dir_b, *s[2], self.to_right)
        self.d2 = remote(self.part(self.left, 0), dir_a, *s[3], self.to_left)
        self.c3 = remote(rel_a, fin_a, *s[4], self.to_right)
        self.d3 = remote(rel_b, fin_b, *s[5], self.to_left)
        for copy in (self.c1, self.d1, self.c2, self.d2):
            copy.start()

    def relay(self):
        rel_a, rel_b = self.bufs[:2]
        self.c1.wait_recv()
        rel_a[...] = (rel_a[...].astype(F32) + self.part(self.right, 0)[...].astype(F32)).astype(BF)
        self.c3.start()
        self.d1.wait_recv()
        rel_b[...] = (rel_b[...].astype(F32) + self.part(self.left, 1)[...].astype(F32)).astype(BF)
        self.d3.start()

    def out_half(self, half):
        index = tuple(pl.ds(2 * half, 2) if a == self.half else ALL for a in self.axes if a != self.over)
        return self.out.at[index]

    def finish(self):
        _, _, dir_a, dir_b, fin_a, fin_b = self.bufs
        self.d2.wait_recv()
        self.c3.wait_recv()
        self.out_half(0)[...] = (
            self.part(self.here, 0)[...].astype(F32) + fin_a[...].astype(F32) + dir_a[...].astype(F32)
        ).astype(BF)
        self.c2.wait_recv()
        self.d3.wait_recv()
        self.out_half(1)[...] = (
            self.part(self.here, 1)[...].astype(F32) + fin_b[...].astype(F32) + dir_b[...].astype(F32)
        ).astype(BF)

    def drain(self):
        for copy in (self.c1, self.d1, self.c2, self.d2, self.c3, self.d3):
            copy.wait_send()


class Unit:
    def __init__(self, src, cols, order, spot, device_at, bufs, send, recv):
        a, b, c = order
        first, second, out1, out2, last = bufs
        rest = tuple(n for n in (0, 1, 2) if n != a)
        self.one = Ring(src, (0, 1, 2), cols, a, b, spot, device_at, first, out1, send, recv, 0)
        self.two = Ring(out1, rest, None, b, c, spot, device_at, second, out2, send, recv, 6)
        self.out2, self.last = out2, last
        self.here = spot[c]
        self.copies = []
        for k in (2, 1, 3):
            there = (self.here + k) % 4
            self.copies.append(
                remote(
                    out2.at[there],
                    last.at[k - 1],
                    send.at[11 + k],
                    recv.at[11 + k],
                    device_at(c, there),
                )
            )

    def start3(self):
        for copy in self.copies:
            copy.start()

    def finish3(self):
        for copy in self.copies:
            copy.wait_recv()
        total = self.out2[self.here].astype(F32)
        for k in range(3):
            total = total + self.last[k].astype(F32)
        return total

    def drain(self):
        self.one.drain()
        self.two.drain()
        for copy in self.copies:
            copy.wait_send()


def unit_scratch(width, order):
    a, b, c = order
    rest = tuple(n for n in (0, 1, 2) if n != a)
    one = tuple(2 if n == b else 4 for n in rest)
    return (
        [pltpu.VMEM(one + (16, width), BF)] * 6
        + [pltpu.VMEM((2, 16, width), BF)] * 6
        + [pltpu.VMEM((4, 4, 16, width), BF), pltpu.VMEM((4, 16, width), BF), pltpu.VMEM((3, 16, width), BF)]
    )


FIXED = (
    ("og", (256, 1024), BF),
    ("dn", (2048, 1024), BF),
    ("gig", (256, 1024), BF),
    ("pw", (1024, 1024), BF),
    ("emb", (256, 1024), BF),
    ("up", (1024, 2048), BF),
    ("og2", (2, 256, 1024), BF),
    ("slot", (8, 32, 1024), BF),
    ("dh", (8, 256, 256), F32),
    ("norm", (256, 1024), F32),
    ("scale", (256, 128), F32),
    ("r2", (2, 256, 1024), BF),
    ("hot", (256, 256), BF),
    ("ht", (2, 1024, 256), BF),
    ("hr", (1024, 256), BF),
    ("dat", (2, 1024, 256), BF),
    ("dar", (1024, 256), BF),
    ("da", (256, 2048), BF),
    ("dr", (256, 1024), F32),
    ("du", (256, 1024), BF),
    ("dut", (1024, 256), BF),
    ("dp", (4, 4, 4, 16, 1024), BF),
    ("upart", (4, 4, 4, 16, 1024), BF),
    ("mp", (2, 4, 4, 4, 16, M_WIDTH), BF),
    ("mr", (4, 4, 4, 16, M_WIDTH), BF),
    ("gog", (8, 32, 1024), BF),
    ("agb", (2, 4, 4, 4, 16, 256), BF),
    ("gp", (4, 4, 8, 1024), F32),
)


def kernel(*refs):
    ids, go_h, gig_h, og_h, pw_h, emb_h, gain, up_h, dn_h = refs[:9]
    gog_o, embg_o, embl_o, gain_o, proj_o, up_o, down_o = refs[9:16]
    rest = list(refs[16:])
    buf = {name: rest.pop(0) for name, _, _ in FIXED}
    unit_bufs = []
    for _ in ALL_UNITS:
        mine = [rest.pop(0) for _ in range(15)]
        unit_bufs.append((mine[:6], mine[6:12], mine[12], mine[13], mine[14]))
    load_sem, x_send, x_recv, a_send, a_recv, b_send, b_recv, u_send, u_recv, g_send, g_recv, q_send, q_recv = rest
    og, dn, gig, pw, emb, up = (buf[n] for n in ("og", "dn", "gig", "pw", "emb", "up"))
    og2, slot, dh, norm, scale, r2 = (buf[n] for n in ("og2", "slot", "dh", "norm", "scale", "r2"))
    hot, ht, hr, dat, dar, da = (buf[n] for n in ("hot", "ht", "hr", "dat", "dar", "da"))
    dr, du, dut, dp, upart, mp = (buf[n] for n in ("dr", "du", "dut", "dp", "upart", "mp"))
    mr, gog, agb, gp = (buf[n] for n in ("mr", "gog", "agb", "gp"))

    seq = lax.axis_index("seq")
    tp = lax.axis_index("tp")
    core = seq % 2
    other = 1 - core
    x = seq // 4
    y = (seq // 2) % 2 * 2 + tp % 2
    z = tp // 2
    spot = (x, y, z)

    def device(px, py, pz, pc):
        return ((px * 2 + py // 2) * 2 + pc, pz * 2 + py % 2)

    def device_at(axis, place):
        where = list(spot)
        where[axis] = place
        return device(*where, core)

    partner = device(x, y, z, other)

    barrier = pltpu.get_barrier_semaphore()
    pl.semaphore_signal(barrier, inc=1, device_id=partner, device_id_type=MESH)
    for k in range(1, 8):
        pl.semaphore_signal(barrier, inc=1, device_id=(seq, (tp + k) % 8), device_id_type=MESH)
    for axis in range(3):
        for k in range(1, 4):
            pl.semaphore_signal(
                barrier, inc=1, device_id=device_at(axis, (spot[axis] + k) % 4), device_id_type=MESH
            )
    loads = {}
    for n, (name, src, dst) in enumerate(
        (
            ("og", og_h, og),
            ("dn", dn_h, dn),
            ("gig", gig_h, gig),
            ("pw", pw_h, pw),
            ("emb", emb_h, emb),
            ("up", up_h, up),
            ("own", go_h.at[tp], slot.at[tp]),
        )
    ):
        loads[name] = pltpu.make_async_copy(src, dst, load_sem.at[n])
        loads[name].start()
    pl.semaphore_wait(barrier, 17)

    fetch = [
        remote(go_h.at[(tp + k) % 8], slot.at[tp], a_send.at[k - 1], a_recv.at[k - 1], (seq, (tp + k) % 8))
        for k in range(1, 8)
    ]
    for copy in fetch:
        copy.start()

    def swap(n, src, dst):
        copy = remote(src, dst, x_send.at[n], x_recv.at[n], partner)
        copy.start()
        return copy

    loads["og"].wait()
    row, col = iota((256, 256), 0), iota((256, 256), 1)
    perm = (col == 8 * (row % 32) + row // 32).astype(BF)
    og2[0] = mm(perm, og[...]).astype(BF)
    x_og = swap(0, og2.at[0], og2.at[1])

    loads["dn"].wait()

    def dh_step(n, carry):
        at = pl.ds(pl.multiple_of(n * 256, 256), 256)
        dh[n] = mm_nt(og2[0], dn[at, :])
        return carry

    lax.fori_loop(0, 8, dh_step, 0)

    ids_v = ids[...]
    own_id = jnp.sum(jnp.where(iota((8, 256), 0) == tp, ids_v, 0), axis=0, keepdims=True)
    hot_own = (row == own_id).astype(BF)
    pick = (row == tp * 32 + col % 32).astype(BF)
    ids_here = mm(ids_v.astype(F32).astype(BF), pick)
    col8 = iota((8, 256), 1)
    prev = jnp.sum(jnp.where(iota((8, 256), 0) == col8 // 32 - 1, ids_here, 0.0), axis=0, keepdims=True)
    prev_id = jnp.where(iota((1, 256), 1) < 32, -1, prev.astype(jnp.int32))
    hot[...] = (row == prev_id).astype(BF)

    def put_table(n, value, first):
        block = value.astype(BF).reshape(4, 2, 2, 16, 256)
        for c in range(2):
            for yh in range(2):
                for yl in range(2):
                    mp[c, :, yh * 2 + yl, n, :, pl.ds(first, 128)] = block[:, yh, c, :, yl * 128 : yl * 128 + 128]

    loads["gig"].wait()
    for n in range(4):
        put_table(n, mm(hot_own, gig[:, n * 256 : n * 256 + 256]), 640)
    x_eg = swap(1, mp.at[other, :, :, :, :, pl.ds(640, 128)], mr.at[:, :, :, :, pl.ds(640, 128)])

    loads["pw"].wait()
    loads["emb"].wait()
    loads["own"].wait()
    for copy in fetch:
        copy.wait_recv()

    square = jnp.zeros((256, 1), F32)
    slot_v = slot[...].reshape(256, 1024)
    for n in range(4):
        at = slice(n * 256, n * 256 + 256)
        u_part = mm(slot_v, pw[:, at]) + mm_tn(hot[...], emb[:, at])
        norm[:, at] = u_part
        square = square + jnp.sum(u_part * u_part, axis=1, keepdims=True)
    scale_v = lax.rsqrt(square * (1.0 / 1024.0) + 1e-05)
    scale[...] = jnp.broadcast_to(scale_v, (256, 128))
    for n in range(4):
        at = slice(n * 256, n * 256 + 256)
        normed = norm[:, at] * scale_v
        norm[:, at] = normed
        r2[0, :, at] = (normed * gain[:, at]).astype(BF)
    x_r = swap(2, r2.at[0], r2.at[1])

    loads["up"].wait()

    def ff_step(k, carry):
        at = pl.ds(pl.multiple_of(k * 256, 256), 256)
        rows = pl.ds(pl.multiple_of(k * 128, 128), 128)
        a = mm(r2[0], up[:, at])
        sig = jax.nn.sigmoid(a)
        h_t = (a * sig).astype(BF).T
        ht[0, rows, :] = h_t[:128]
        ht[1, rows, :] = h_t[128:]
        da_v = (dh[k] * sig * (1.0 + a * (1.0 - sig))).astype(BF)
        da[:, at] = da_v
        da_t = da_v.T
        dat[0, rows, :] = da_t[:128]
        dat[1, rows, :] = da_t[128:]
        return carry

    lax.fori_loop(0, 8, ff_step, 0)
    x_h = swap(3, ht.at[other], hr)
    x_da = swap(4, dat.at[other], dar)

    def units(src, table, first):
        return [
            Unit(src, cols_of(t), t[2], spot, device_at, unit_bufs[first + i], u_send.at[first + i], u_recv.at[first + i])
            for i, t in enumerate(table)
        ]

    def cols_of(entry):
        return entry[0], entry[1]

    d_units = units(dp, D_UNITS, 0)
    m_units = units(mr, M_UNITS, 3)
    u_units = units(upart, U_UNITS, 6)

    def big(lhs, lhs_far, rhs, out, table):
        done = 0
        for n in range(4):
            at = slice(n * 256, n * 256 + 256)

            def step(g, carry):
                rows = pl.ds(pl.multiple_of(g * 512, 512), 512)
                v = mm(lhs[core, rows, :], rhs[0, :, at]) + mm(lhs_far[rows, :], rhs[1, :, at])
                v = v.astype(BF).reshape(2, 2, 4, 2, 16, 256)
                for xx in range(2):
                    for yh in range(2):
                        for yl in range(2):
                            out[2 * g + xx, yh * 2 + yl, :, :, at] = v[xx, yh, :, yl]
                return carry

            lax.fori_loop(0, 2, step, 0)
            while done < 3 and table[done].one.cols[0] + table[done].one.cols[1] <= n * 256 + 256:
                table[done].one.start()
                done += 1

    x_og.wait_recv()
    x_h.wait_recv()
    big(ht, hr, og2, dp, d_units)

    for n in range(4):
        at = slice(n * 256, n * 256 + 256)
        dr[:, at] = mm_nt(da[...], up[at, :])
    for unit in d_units:
        unit.one.relay()

    gain_v = gain[...]

    def du_step(i, total):
        rows = pl.ds(pl.multiple_of(i * 32, 32), 32)
        dr_v = dr[rows, :]
        normed = norm[rows, :]
        product = dr_v * normed
        dn_v = dr_v * gain_v
        mean = jnp.sum(product * gain_v, axis=1, keepdims=True) * (1.0 / 1024.0)
        du_v = og2[0, rows, :].astype(F32) + scale[rows, 0:1] * (dn_v - normed * mean)
        du[rows, :] = du_v.astype(BF)
        return total + jnp.sum(product.reshape(4, 8, 1024), axis=0)

    gain_part = lax.fori_loop(0, 8, du_step, jnp.zeros((8, 1024), F32))
    gp[0, core] = gain_part
    x_g = swap(5, gp.at[0, core], gp.at[0, core])

    for n in range(4):
        at = slice(n * 256, n * 256 + 256)
        dut[at, :] = du[:, at].T

    for n in range(4):
        put_table(n, mm(hot[...], du[:, n * 256 : n * 256 + 256]), 512)
    x_el = swap(6, mp.at[other, :, :, :, :, pl.ds(512, 128)], mr.at[:, :, :, :, pl.ds(512, 128)])

    def proj_step(g, carry):
        rows = pl.ds(pl.multiple_of(g * 256, 256), 256)
        for n in range(2):
            lo, hi = slice(n * 256, n * 256 + 256), slice(512 + n * 256, 768 + n * 256)
            v_lo = mm(dut[rows, :], slot[:, :, lo].reshape(256, 256)).reshape(2, 2, 4, 2, 8, 256)
            v_hi = mm(dut[rows, :], slot[:, :, hi].reshape(256, 256)).reshape(2, 2, 4, 2, 8, 256)
            v = jnp.concatenate([v_lo, v_hi], axis=4).astype(BF)
            for c in range(2):
                for yh in range(2):
                    for yl in range(2):
                        mp[c, g, yh * 2 + yl, :, :, lo] = v[yh, c, :, yl]
        return carry

    lax.fori_loop(0, 4, proj_step, 0)
    x_p = swap(7, mp.at[other, :, :, :, :, pl.ds(0, 512)], mr.at[:, :, :, :, pl.ds(0, 512)])

    for n in range(4):
        at = slice(n * 256, n * 256 + 256)
        gog[:, :, at] = mm_nt(du[...], pw[at, :]).astype(BF).reshape(8, 32, 256)
    own_back = pltpu.make_async_copy(gog.at[tp], gog_o.at[tp], load_sem.at[7])
    own_back.start()
    back = [
        remote(gog.at[(tp + k) % 8], gog_o.at[tp], b_send.at[k - 1], b_recv.at[k - 1], (seq, (tp + k) % 8))
        for k in range(1, 8)
    ]

    x_eg.wait_recv()
    x_el.wait_recv()
    x_p.wait_recv()

    def join_step(i, carry):
        mr[i] = (mr[i].astype(F32) + mp[core, i].astype(F32)).astype(BF)
        return carry

    lax.fori_loop(0, 4, join_step, 0)
    for unit in m_units:
        unit.one.start()
    for copy in back:
        copy.start()

    def gain_swap(step):
        axis = step - 1
        place = spot[axis]
        copies = [
            remote(
                gp.at[step, place],
                gp.at[step, place],
                g_send.at[axis * 3 + k - 1],
                g_recv.at[axis * 3 + k - 1],
                device_at(axis, (place + k) % 4),
            )
            for k in range(1, 4)
        ]
        for copy in copies:
            copy.start()
        return copies

    x_g.wait_recv()
    x_g.wait_send()
    gp[1, x] = gp[0, 0] + gp[0, 1]
    g1 = gain_swap(1)

    for unit in d_units:
        unit.one.finish()
        unit.two.start()
    x_r.wait_recv()
    x_da.wait_recv()
    for unit in m_units:
        unit.one.relay()
    big(dat, dar, r2, upart, u_units)
    for unit in d_units:
        unit.two.relay()

    def gain_join(step, copies):
        for copy in copies:
            copy.wait_recv()
        for copy in copies:
            copy.wait_send()
        return gp[step, 0] + gp[step, 1] + gp[step, 2] + gp[step, 3]

    gp[2, y] = gain_join(1, g1)
    g2 = gain_swap(2)
    for unit in m_units:
        unit.one.finish()
        unit.two.start()
    for unit in d_units:
        unit.two.finish()
        unit.start3()
    for unit in u_units:
        unit.one.relay()
    for unit in m_units:
        unit.two.relay()
    for unit in m_units:
        unit.two.finish()
        unit.start3()
    gp[3, z] = gain_join(2, g2)
    g3 = gain_swap(3)
    for i, unit in enumerate(d_units):
        down_o[:, pl.ds(*cols_of(D_UNITS[i]))] = unit.finish3()
    for unit in u_units:
        unit.one.finish()
        unit.two.start()

    table = m_units[0].finish3()
    agb[core, x, y, z] = table.astype(BF)
    gather = []

    def spread(base, axis, ref):
        copies = [
            remote(ref, ref, q_send.at[base + k - 1], q_recv.at[base + k - 1], device_at(axis, (spot[axis] + k) % 4))
            for k in range(1, 4)
        ]
        for copy in copies:
            copy.start()
        gather.extend(copies)
        return copies

    q1 = spread(0, 2, agb.at[core, x, y, z])
    for i in (1, 2):
        first = M_UNITS[i][0]
        value = m_units[i].finish3()
        proj_o[:, pl.ds(first, 256)] = value[:8]
        proj_o[:, pl.ds(512 + first, 256)] = value[8:]
    for unit in u_units:
        unit.two.relay()
    for copy in q1:
        copy.wait_recv()
    q2 = spread(3, 1, agb.at[core, x, y])
    for unit in u_units:
        unit.two.finish()
        unit.start3()
    for copy in q2:
        copy.wait_recv()
    q3 = spread(6, 0, agb.at[core, x])
    total = gain_join(3, g3)
    gain_o[...] = jnp.sum(total, axis=0, keepdims=True)
    for i, unit in enumerate(u_units):
        up_o[:, pl.ds(*cols_of(U_UNITS[i]))] = unit.finish3()
    for copy in q3:
        copy.wait_recv()
    x_ag = swap(8, agb.at[core], agb.at[core])

    def write_out(c):
        for px in range(4):
            for py in range(4):
                rows = pl.ds(pl.multiple_of(((px * 2 + py // 2) * 2 + c) * 16, 16), 16)
                for pz in range(4):
                    at = (pz * 2 + py % 2) * 128
                    value = agb[c, px, py, pz].astype(F32)
                    embl_o[rows, at : at + 128] = value[:, :128]
                    embg_o[rows, at : at + 128] = value[:, 128:]

    write_out(core)
    x_ag.wait_recv()
    write_out(other)
    for copy in back:
        copy.wait_recv()
    own_back.wait()
    for unit in d_units + m_units + u_units:
        unit.drain()
    for copy in fetch + back + gather + [x_og, x_eg, x_r, x_h, x_da, x_el, x_p, x_ag]:
        copy.wait_send()


def on_device(
    byte_ids,
    global_out,
    global_in_grad,
    out_grad,
    proj_weight,
    emb_local,
    norm_gain,
    up_weight,
    down_weight,
):
    scratch = [pltpu.VMEM(shape, kind) for _, shape, kind in FIXED]
    for _, width, order in ALL_UNITS:
        scratch += unit_scratch(width, order)
    dma = pltpu.SemaphoreType.DMA
    scratch += [dma((8,)), dma((9,)), dma((9,)), dma((7,)), dma((7,)), dma((7,)), dma((7,))]
    scratch += [dma((9, 15)), dma((9, 15)), dma((9,)), dma((9,)), dma((9,)), dma((9,))]
    vmem = pl.BlockSpec(memory_space=pltpu.VMEM)
    anywhere = pl.BlockSpec(memory_space=pl.ANY)
    out = jax.ShapeDtypeStruct
    gog, embg, embl, gain, proj, up, down = pl.pallas_call(
        kernel,
        out_shape=(
            out((8, 32, 1024), BF),
            out((256, 1024), F32),
            out((256, 1024), F32),
            out((1, 1024), F32),
            out((8, 1024), F32),
            out((16, 1024), F32),
            out((16, 1024), F32),
        ),
        in_specs=[vmem] + [anywhere] * 5 + [vmem] + [anywhere] * 2,
        out_specs=[anywhere] + [vmem] * 6,
        scratch_shapes=scratch,
        compiler_params=pltpu.CompilerParams(
            collective_id=0, has_side_effects=True, vmem_limit_bytes=60 * 1024 * 1024
        ),
    )(
        byte_ids.T,
        global_out.reshape(8, 32, 1024),
        global_in_grad,
        out_grad,
        proj_weight,
        emb_local,
        norm_gain.reshape(1, 1024),
        up_weight,
        down_weight,
    )
    return gog.reshape(256, 1024), embg, embl, gain.reshape(1024), proj.T, up.T, down


def solution(mesh):
    placed = (
        P("seq", None),
        P("seq", "tp"),
        P("seq", "tp"),
        P(("seq", "tp"), None),
        P(),
        P(),
        P(),
        P(),
        P(),
    )
    return jax.shard_map(
        on_device,
        mesh=mesh,
        in_specs=placed,
        out_specs=(
            P("seq", "tp"),
            P(),
            P(),
            P(),
            P(None, ("seq", "tp")),
            P(None, ("seq", "tp")),
            P(("seq", "tp"), None),
        ),
        check_vma=False,
    )
```

```python
import jax
import jax.numpy as jnp
from jax import lax
from jax.experimental import pallas as pl
from jax.experimental.pallas import tpu as pltpu
from jax.sharding import PartitionSpec as P

BF = jnp.bfloat16
F32 = jnp.float32
MESH = pl.DeviceIdType.MESH
ALL = slice(None)
D_UNITS = ((0, 384, (0, 1, 2)), (384, 384, (1, 2, 0)), (768, 256, (2, 0, 1)))
U_UNITS = ((0, 384, (0, 1, 2)), (384, 256, (1, 2, 0)), (640, 384, (2, 0, 1)))
P_UNITS = ((0, 256, (0, 1, 2)), (256, 128, (1, 2, 0)), (384, 128, (2, 0, 1)))
ALL_UNITS = D_UNITS + U_UNITS + P_UNITS
FAR_FIRST = (2, 1, 3)


def mm(a, b):
    return lax.dot_general(a, b, (((1,), (0,)), ((), ())), preferred_element_type=F32)


def mm_nt(a, b):
    return lax.dot_general(a, b, (((1,), (1,)), ((), ())), preferred_element_type=F32)


def mm_tn(a, b):
    return lax.dot_general(a, b, (((0,), (0,)), ((), ())), preferred_element_type=F32)


def iota(shape, dim):
    return lax.broadcasted_iota(jnp.int32, shape, dim)


def remote(src, dst, send, recv, device):
    return pltpu.make_async_remote_copy(
        src_ref=src, dst_ref=dst, send_sem=send, recv_sem=recv, device_id=device, device_id_type=MESH
    )


class Ring:
    def __init__(self, src, axes, cols, over, half, spot, device_at, bufs, out, send, recv, base):
        self.src, self.axes, self.cols, self.over, self.half = src, axes, cols, over, half
        self.bufs, self.out, self.spot = bufs, out, spot
        here = spot[over]
        self.here, self.right, self.left, self.far = here, (here + 1) % 4, (here + 3) % 4, (here + 2) % 4
        self.to_right = device_at(over, self.right)
        self.to_left = device_at(over, self.left)
        self.sems = [(send.at[base + i], recv.at[base + i]) for i in range(6)]

    def part(self, place, half):
        index = tuple(
            place if a == self.over else pl.ds(2 * half, 2) if a == self.half else ALL for a in self.axes
        )
        cols = ALL if self.cols is None else pl.ds(*self.cols)
        return self.src.at[index + (ALL, cols)]

    def start(self):
        rel_a, rel_b, dir_a, dir_b, fin_a, fin_b = self.bufs
        s = self.sems
        self.c1 = remote(self.part(self.far, 0), rel_a, *s[0], self.to_right)
        self.d1 = remote(self.part(self.far, 1), rel_b, *s[1], self.to_left)
        self.c2 = remote(self.part(self.right, 1), dir_b, *s[2], self.to_right)
        self.d2 = remote(self.part(self.left, 0), dir_a, *s[3], self.to_left)
        self.c3 = remote(rel_a, fin_a, *s[4], self.to_right)
        self.d3 = remote(rel_b, fin_b, *s[5], self.to_left)
        for copy in (self.c1, self.d1, self.c2, self.d2):
            copy.start()

    def relay(self):
        rel_a, rel_b = self.bufs[:2]
        self.c1.wait_recv()
        rel_a[...] = (rel_a[...].astype(F32) + self.part(self.right, 0)[...].astype(F32)).astype(BF)
        self.c3.start()
        self.d1.wait_recv()
        rel_b[...] = (rel_b[...].astype(F32) + self.part(self.left, 1)[...].astype(F32)).astype(BF)
        self.d3.start()

    def out_half(self, half):
        index = tuple(pl.ds(2 * half, 2) if a == self.half else ALL for a in self.axes if a != self.over)
        return self.out.at[index]

    def finish(self):
        _, _, dir_a, dir_b, fin_a, fin_b = self.bufs
        self.d2.wait_recv()
        self.c3.wait_recv()
        self.out_half(0)[...] = (
            self.part(self.here, 0)[...].astype(F32) + fin_a[...].astype(F32) + dir_a[...].astype(F32)
        ).astype(BF)
        self.c2.wait_recv()
        self.d3.wait_recv()
        self.out_half(1)[...] = (
            self.part(self.here, 1)[...].astype(F32) + fin_b[...].astype(F32) + dir_b[...].astype(F32)
        ).astype(BF)

    def drain(self):
        for copy in (self.c1, self.d1, self.c2, self.d2, self.c3, self.d3):
            copy.wait_send()


class Unit:
    def __init__(self, src, cols, order, spot, device_at, bufs, send, recv):
        a, b, c = order
        first, second, out1, out2, last = bufs
        rest = tuple(n for n in (0, 1, 2) if n != a)
        self.one = Ring(src, (0, 1, 2), cols, a, b, spot, device_at, first, out1, send, recv, 0)
        self.two = Ring(out1, rest, None, b, c, spot, device_at, second, out2, send, recv, 6)
        self.out2, self.last = out2, last
        self.here = spot[c]
        self.copies = []
        for k in (2, 1, 3):
            there = (self.here + k) % 4
            self.copies.append(
                remote(
                    out2.at[there],
                    last.at[k - 1],
                    send.at[11 + k],
                    recv.at[11 + k],
                    device_at(c, there),
                )
            )

    def start3(self):
        for copy in self.copies:
            copy.start()

    def finish3(self):
        for copy in self.copies:
            copy.wait_recv()
        total = self.out2[self.here].astype(F32)
        for k in range(3):
            total = total + self.last[k].astype(F32)
        return total

    def drain(self):
        self.one.drain()
        self.two.drain()
        for copy in self.copies:
            copy.wait_send()


class Table:
    def __init__(self, bufs, gathered, spot, core, device_at, partner, send, recv):
        src, one, two, recv1, recv2, recv3 = bufs
        self.src, self.out = (src, one, two), (one, two, None)
        self.recv = (recv1, recv2, recv3)
        self.spot, self.gathered = spot, gathered
        x, y, z = spot
        own = (gathered.at[core, x, y, z], gathered.at[core, x, y], gathered.at[core, x])
        self.scatter, self.spread = [], []
        for step in range(3):
            self.scatter.append(
                [
                    remote(
                        self.src[step].at[(spot[step] + k) % 4],
                        self.recv[step].at[k - 1],
                        send.at[step * 3 + k - 1],
                        recv.at[step * 3 + k - 1],
                        device_at(step, (spot[step] + k) % 4),
                    )
                    for k in FAR_FIRST
                ]
            )
            axis = 2 - step
            self.spread.append(
                [
                    remote(
                        own[step],
                        own[step],
                        send.at[9 + step * 3 + k - 1],
                        recv.at[9 + step * 3 + k - 1],
                        device_at(axis, (spot[axis] + k) % 4),
                    )
                    for k in FAR_FIRST
                ]
            )
        self.spread.append([remote(gathered.at[core], gathered.at[core], send.at[18], recv.at[18], partner)])
        self.place = gathered.at[core, x, y, z]

    def start(self, step):
        for copy in self.scatter[step] if step < 3 else self.spread[step - 3]:
            copy.start()

    def finish(self, step):
        for copy in self.scatter[step] if step < 3 else self.spread[step - 3]:
            copy.wait_recv()
        if step < 3:
            total = self.src[step][self.spot[step]].astype(F32)
            for k in range(3):
                total = total + self.recv[step][k].astype(F32)
            if step == 2:
                self.place[...] = total.astype(BF)
            else:
                self.out[step][...] = total.astype(BF)

    def drain(self):
        for copies in self.scatter + self.spread:
            for copy in copies:
                copy.wait_send()


def unit_scratch(width, order):
    a, b, c = order
    rest = tuple(n for n in (0, 1, 2) if n != a)
    one = tuple(2 if n == b else 4 for n in rest)
    return (
        [pltpu.VMEM(one + (16, width), BF)] * 6
        + [pltpu.VMEM((2, 16, width), BF)] * 6
        + [pltpu.VMEM((4, 4, 16, width), BF), pltpu.VMEM((4, 16, width), BF), pltpu.VMEM((3, 16, width), BF)]
    )


FIXED = (
    ("og", (256, 1024), BF),
    ("dn", (2048, 1024), BF),
    ("gig", (256, 1024), BF),
    ("pw", (1024, 1024), BF),
    ("emb", (256, 1024), BF),
    ("up", (1024, 2048), BF),
    ("og2", (2, 256, 1024), BF),
    ("slot", (8, 32, 1024), BF),
    ("dh", (8, 256, 256), F32),
    ("norm", (256, 1024), F32),
    ("scale", (256, 128), F32),
    ("r2", (2, 256, 1024), BF),
    ("hot", (256, 256), BF),
    ("ht", (2, 1024, 256), BF),
    ("hr", (1024, 256), BF),
    ("dat", (2, 1024, 256), BF),
    ("dar", (1024, 256), BF),
    ("da", (256, 2048), BF),
    ("dr", (256, 1024), F32),
    ("du", (256, 1024), BF),
    ("dut", (1024, 256), BF),
    ("dp", (4, 4, 4, 16, 1024), BF),
    ("upart", (4, 4, 4, 16, 1024), BF),
    ("pp", (2, 4, 4, 4, 16, 512), BF),
    ("pr", (4, 4, 4, 16, 512), BF),
    ("gog", (8, 32, 1024), BF),
    ("gp", (4, 4, 1, 1024), F32),
)
TABLE = (
    ("part", (2, 4, 4, 4, 16, 128)),
    ("src", (4, 4, 4, 16, 128)),
    ("one", (4, 4, 16, 128)),
    ("two", (4, 16, 128)),
    ("recv1", (3, 4, 4, 16, 128)),
    ("recv2", (3, 4, 16, 128)),
    ("recv3", (3, 16, 128)),
)
N_SEMS = {"load": 8, "x": 20, "a": 7, "b": 7, "g": 9, "tg": 19, "tl": 19}


def kernel(*refs):
    ids, go_h, gig_h, og_h, pw_h, emb_h, gain, up_h, dn_h = refs[:9]
    gog_o, table_g, table_l, gain_o, proj_o, up_o, down_o = refs[9:16]
    rest = list(refs[16:])
    buf = {name: rest.pop(0) for name, _, _ in FIXED}
    eg = {name: rest.pop(0) for name, _ in TABLE}
    el = {name: rest.pop(0) for name, _ in TABLE}
    unit_bufs = []
    for _ in ALL_UNITS:
        mine = [rest.pop(0) for _ in range(15)]
        unit_bufs.append((mine[:6], mine[6:12], mine[12], mine[13], mine[14]))
    sems = {name: (rest.pop(0), rest.pop(0)) for name in N_SEMS}
    u_send, u_recv = rest
    load_sem = sems["load"][0]
    (x_send, x_recv), (a_send, a_recv), (b_send, b_recv), (g_send, g_recv) = (sems[n] for n in ("x", "a", "b", "g"))
    og, dn, gig, pw, emb, up = (buf[n] for n in ("og", "dn", "gig", "pw", "emb", "up"))
    og2, slot, dh, norm, scale, r2 = (buf[n] for n in ("og2", "slot", "dh", "norm", "scale", "r2"))
    hot, ht, hr, dat, dar, da = (buf[n] for n in ("hot", "ht", "hr", "dat", "dar", "da"))
    dr, du, dut, dp, upart, pp = (buf[n] for n in ("dr", "du", "dut", "dp", "upart", "pp"))
    pr, gog, gp = (buf[n] for n in ("pr", "gog", "gp"))

    seq = lax.axis_index("seq")
    tp = lax.axis_index("tp")
    core = seq % 2
    other = 1 - core
    x = seq // 4
    y = (seq // 2) % 2 * 2 + tp % 2
    z = tp // 2
    spot = (x, y, z)

    def device(px, py, pz, pc):
        return ((px * 2 + py // 2) * 2 + pc, pz * 2 + py % 2)

    def device_at(axis, place):
        where = list(spot)
        where[axis] = place
        return device(*where, core)

    partner = device(x, y, z, other)

    barrier = pltpu.get_barrier_semaphore()
    pl.semaphore_signal(barrier, inc=1, device_id=partner, device_id_type=MESH)
    for k in range(1, 8):
        pl.semaphore_signal(barrier, inc=1, device_id=(seq, (tp + k) % 8), device_id_type=MESH)
    for axis in range(3):
        for k in range(1, 4):
            pl.semaphore_signal(
                barrier, inc=1, device_id=device_at(axis, (spot[axis] + k) % 4), device_id_type=MESH
            )
    loads = {}
    for n, (name, src, dst) in enumerate(
        (
            ("og", og_h, og),
            ("dn", dn_h, dn),
            ("gig", gig_h, gig),
            ("pw", pw_h, pw),
            ("emb", emb_h, emb),
            ("up", up_h, up),
            ("own", go_h.at[tp], slot.at[tp]),
        )
    ):
        loads[name] = pltpu.make_async_copy(src, dst, load_sem.at[n])
        loads[name].start()
    pl.semaphore_wait(barrier, 17)

    fetch = [
        remote(go_h.at[(tp + k) % 8], slot.at[tp], a_send.at[k - 1], a_recv.at[k - 1], (seq, (tp + k) % 8))
        for k in range(1, 8)
    ]
    for copy in fetch:
        copy.start()

    def swap(n, src, dst):
        copy = remote(src, dst, x_send.at[n], x_recv.at[n], partner)
        copy.start()
        return copy

    loads["og"].wait()
    row, col = iota((256, 256), 0), iota((256, 256), 1)
    perm = (col == 8 * (row % 32) + row // 32).astype(BF)
    og2[0] = mm(perm, og[...]).astype(BF)
    x_og = swap(0, og2.at[0], og2.at[1])

    loads["dn"].wait()

    def dh_step(n, carry):
        at = pl.ds(pl.multiple_of(n * 256, 256), 256)
        dh[n] = mm_nt(og2[0], dn[at, :])
        return carry

    lax.fori_loop(0, 8, dh_step, 0)

    ids_v = ids[...]
    own_id = jnp.sum(jnp.where(iota((8, 256), 0) == tp, ids_v, 0), axis=0, keepdims=True)
    hot_own = (row == own_id).astype(BF)
    pick = (row == tp * 32 + col % 32).astype(BF)
    ids_here = mm(ids_v.astype(F32).astype(BF), pick)
    col8 = iota((8, 256), 1)
    prev = jnp.sum(jnp.where(iota((8, 256), 0) == col8 // 32 - 1, ids_here, 0.0), axis=0, keepdims=True)
    prev_id = jnp.where(iota((1, 256), 1) < 32, -1, prev.astype(jnp.int32))
    hot[...] = (row == prev_id).astype(BF)

    def table_of(bufs, gathered, name):
        order = tuple(bufs[n] for n in ("src", "one", "two", "recv1", "recv2", "recv3"))
        return Table(order, gathered, spot, core, device_at, partner, *sems[name])

    glob, loc = table_of(eg, table_g, "tg"), table_of(el, table_l, "tl")

    def put_table(part, n, value):
        block = value.astype(BF).reshape(4, 2, 2, 16, 256)
        for c in range(2):
            for yh in range(2):
                for yl in range(2):
                    part[c, :, yh * 2 + yl, n] = block[:, yh, c, :, yl * 128 : yl * 128 + 128]

    def join(part, src):
        def step(i, carry):
            src[i] = (src[i].astype(F32) + part[core, i].astype(F32)).astype(BF)
            return carry

        lax.fori_loop(0, 4, step, 0)

    loads["gig"].wait()
    for n in range(4):
        put_table(eg["part"], n, mm(hot_own, gig[:, n * 256 : n * 256 + 256]))
    x_eg = swap(1, eg["part"].at[other], eg["src"])

    loads["pw"].wait()
    loads["emb"].wait()
    loads["own"].wait()
    x_eg.wait_recv()
    join(eg["part"], eg["src"])
    glob.start(0)
    for copy in fetch:
        copy.wait_recv()

    square = jnp.zeros((256, 1), F32)
    slot_v = slot[...].reshape(256, 1024)
    for n in range(4):
        at = slice(n * 256, n * 256 + 256)
        u_part = mm(slot_v, pw[:, at]) + mm_tn(hot[...], emb[:, at])
        norm[:, at] = u_part
        square = square + jnp.sum(u_part * u_part, axis=1, keepdims=True)
    scale_v = lax.rsqrt(square * (1.0 / 1024.0) + 1e-05)
    scale[...] = jnp.broadcast_to(scale_v, (256, 128))
    for n in range(4):
        at = slice(n * 256, n * 256 + 256)
        normed = norm[:, at] * scale_v
        norm[:, at] = normed
        r2[0, :, at] = (normed * gain[:, at]).astype(BF)
    x_r = swap(2, r2.at[0], r2.at[1])

    loads["up"].wait()
    glob.finish(0)
    glob.start(1)

    def h_swap(j):
        rows = pl.ds(pl.multiple_of(j * 256, 256), 256)
        return remote(ht.at[other, rows], hr.at[rows], x_send.at[8 + j], x_recv.at[8 + j], partner)

    def ff_step(j, carry):
        for k2 in range(2):
            k = j * 2 + k2
            at = pl.ds(pl.multiple_of(k * 256, 256), 256)
            rows = pl.ds(pl.multiple_of(k * 128, 128), 128)
            a = mm(r2[0], up[:, at])
            sig = jax.nn.sigmoid(a)
            h_t = (a * sig).astype(BF).T
            ht[0, rows, :] = h_t[:128]
            ht[1, rows, :] = h_t[128:]
            da_v = (dh[k] * sig * (1.0 + a * (1.0 - sig))).astype(BF)
            da[:, at] = da_v
            da_t = da_v.T
            dat[0, rows, :] = da_t[:128]
            dat[1, rows, :] = da_t[128:]
        h_swap(j).start()
        return carry

    lax.fori_loop(0, 2, ff_step, 0)
    glob.finish(1)
    glob.start(2)
    lax.fori_loop(2, 4, ff_step, 0)

    def units(src, table, first):
        return [
            Unit(src, t[:2], t[2], spot, device_at, unit_bufs[first + i], u_send.at[first + i], u_recv.at[first + i])
            for i, t in enumerate(table)
        ]

    d_units = units(dp, D_UNITS, 0)
    u_units = units(upart, U_UNITS, 3)
    p_units = units(pr, P_UNITS, 6)

    def big(lhs, lhs_far, rhs, out, n):
        at = slice(n * 256, n * 256 + 256)

        def step(g, carry):
            rows = pl.ds(pl.multiple_of(g * 512, 512), 512)
            v = mm(lhs[core, rows, :], rhs[0, :, at]) + mm(lhs_far[rows, :], rhs[1, :, at])
            v = v.astype(BF).reshape(2, 2, 4, 2, 16, 256)
            for xx in range(2):
                for yh in range(2):
                    for yl in range(2):
                        out[2 * g + xx, yh * 2 + yl, :, :, at] = v[xx, yh, :, yl]
            return carry

        lax.fori_loop(0, 2, step, 0)

    x_og.wait_recv()
    for j in range(4):
        h_swap(j).wait_recv()
    x_da = swap(4, dat.at[other], dar)
    big(ht, hr, og2, dp, 0)
    glob.finish(2)
    glob.start(3)
    big(ht, hr, og2, dp, 1)
    d_units[0].one.start()
    big(ht, hr, og2, dp, 2)
    d_units[1].one.start()
    big(ht, hr, og2, dp, 3)
    d_units[2].one.start()

    for n in range(4):
        at = slice(n * 256, n * 256 + 256)
        dr[:, at] = mm_nt(da[...], up[at, :])
    glob.finish(3)
    glob.start(4)
    gain_v = gain[...]

    def du_step(i, total):
        rows = pl.ds(pl.multiple_of(i * 32, 32), 32)
        dr_v = dr[rows, :]
        normed = norm[rows, :]
        product = dr_v * normed
        dn_v = dr_v * gain_v
        mean = jnp.sum(product * gain_v, axis=1, keepdims=True) * (1.0 / 1024.0)
        du_v = og2[0, rows, :].astype(F32) + scale[rows, 0:1] * (dn_v - normed * mean)
        du[rows, :] = du_v.astype(BF)
        return total + jnp.sum(product.reshape(4, 8, 1024), axis=0)

    gain_part = lax.fori_loop(0, 8, du_step, jnp.zeros((8, 1024), F32))
    gp[0, core] = jnp.sum(gain_part, axis=0, keepdims=True)
    x_g = swap(5, gp.at[0, core], gp.at[0, core])
    for n in range(4):
        put_table(el["part"], n, mm(hot[...], du[:, n * 256 : n * 256 + 256]))
    x_el = swap(6, el["part"].at[other], el["src"])
    for unit in d_units:
        unit.one.relay()
    for n in range(4):
        at = slice(n * 256, n * 256 + 256)
        dut[at, :] = du[:, at].T
    glob.finish(4)
    glob.start(5)

    x_r.wait_recv()
    x_da.wait_recv()
    big(dat, dar, r2, upart, 0)
    x_el.wait_recv()
    join(el["part"], el["src"])
    loc.start(0)
    big(dat, dar, r2, upart, 1)
    u_units[0].one.start()
    big(dat, dar, r2, upart, 2)
    u_units[1].one.start()
    big(dat, dar, r2, upart, 3)
    u_units[2].one.start()

    def gain_swap(step):
        axis = step - 1
        place = spot[axis]
        copies = [
            remote(
                gp.at[step, place],
                gp.at[step, place],
                g_send.at[axis * 3 + k - 1],
                g_recv.at[axis * 3 + k - 1],
                device_at(axis, (place + k) % 4),
            )
            for k in FAR_FIRST
        ]
        for copy in copies:
            copy.start()
        return copies

    def gain_join(step, copies):
        for copy in copies:
            copy.wait_recv()
        for copy in copies:
            copy.wait_send()
        return gp[step, 0] + gp[step, 1] + gp[step, 2] + gp[step, 3]

    x_g.wait_recv()
    x_g.wait_send()
    gp[1, x] = gp[0, 0] + gp[0, 1]
    g1 = gain_swap(1)
    for unit in d_units:
        unit.one.finish()
        unit.two.start()

    def proj_step(g, carry):
        rows = pl.ds(pl.multiple_of(g * 256, 256), 256)
        for n in range(2):
            lo, hi = slice(n * 256, n * 256 + 256), slice(512 + n * 256, 768 + n * 256)
            v_lo = mm(dut[rows, :], slot[:, :, lo].reshape(256, 256)).reshape(2, 2, 4, 2, 8, 256)
            v_hi = mm(dut[rows, :], slot[:, :, hi].reshape(256, 256)).reshape(2, 2, 4, 2, 8, 256)
            v = jnp.concatenate([v_lo, v_hi], axis=4).astype(BF)
            for c in range(2):
                for yh in range(2):
                    for yl in range(2):
                        pp[c, g, yh * 2 + yl, :, :, lo] = v[yh, c, :, yl]
        return carry

    lax.fori_loop(0, 4, proj_step, 0)
    x_p = swap(7, pp.at[other], pr)
    loc.finish(0)
    loc.start(1)
    glob.finish(5)
    glob.start(6)
    for n in range(4):
        at = slice(n * 256, n * 256 + 256)
        gog[:, :, at] = mm_nt(du[...], pw[at, :]).astype(BF).reshape(8, 32, 256)
    own_back = pltpu.make_async_copy(gog.at[tp], gog_o.at[tp], load_sem.at[7])
    own_back.start()
    back = [
        remote(gog.at[(tp + k) % 8], gog_o.at[tp], b_send.at[k - 1], b_recv.at[k - 1], (seq, (tp + k) % 8))
        for k in range(1, 8)
    ]
    x_p.wait_recv()
    join(pp, pr)
    for unit in p_units:
        unit.one.start()
    for unit in u_units:
        unit.one.relay()
    gp[2, y] = gain_join(1, g1)
    g2 = gain_swap(2)
    loc.finish(1)
    loc.start(2)
    for unit in d_units:
        unit.two.relay()
    for unit in p_units:
        unit.one.relay()
    loc.finish(2)
    loc.start(3)
    for unit in u_units:
        unit.one.finish()
        unit.two.start()
    gp[3, z] = gain_join(2, g2)
    g3 = gain_swap(3)
    for unit in d_units:
        unit.two.finish()
        unit.start3()
    loc.finish(3)
    loc.start(4)
    for unit in p_units:
        unit.one.finish()
        unit.two.start()
    for copy in back:
        copy.start()
    for unit in u_units:
        unit.two.relay()
    loc.finish(4)
    loc.start(5)
    for unit in p_units:
        unit.two.relay()
    for i, unit in enumerate(d_units):
        down_o[:, pl.ds(*D_UNITS[i][:2])] = unit.finish3()
    for unit in u_units:
        unit.two.finish()
        unit.start3()
    for unit in p_units:
        unit.two.finish()
        unit.start3()
    gain_o[...] = gain_join(3, g3)
    loc.finish(5)
    loc.start(6)
    for i, unit in enumerate(u_units):
        up_o[:, pl.ds(*U_UNITS[i][:2])] = unit.finish3()
    for i, unit in enumerate(p_units):
        first, width, _ = P_UNITS[i]
        value = unit.finish3()
        proj_o[:, pl.ds(first, width)] = value[:8]
        proj_o[:, pl.ds(512 + first, width)] = value[8:]
    glob.finish(6)
    for copy in back:
        copy.wait_recv()
    own_back.wait()
    loc.finish(6)
    glob.drain()
    loc.drain()
    for unit in d_units + u_units + p_units:
        unit.drain()
    for copy in fetch + back + [x_og, x_eg, x_r, x_da, x_el, x_p] + [h_swap(j) for j in range(4)]:
        copy.wait_send()


def finish(gog, table_g, table_l, gain, proj, up, down, gog_o, embg_o, embl_o, gain_o, proj_o, up_o, down_o, embg, embl, sem):
    pairs = ((gog, gog_o), (gain, gain_o), (proj, proj_o), (up, up_o), (down, down_o))
    copies = [pltpu.make_async_copy(src, dst, sem.at[n]) for n, (src, dst) in enumerate(pairs)]
    for copy in copies:
        copy.start()
    for n, (table, value, out) in enumerate(((table_g, embg, embg_o), (table_l, embl, embl_o))):
        for row in range(16):
            px, yh, c = row // 4, row // 2 % 2, row % 2
            for col in range(8):
                pz, yl = col // 2, col % 2
                value[row * 16 : row * 16 + 16, col * 128 : col * 128 + 128] = table[c, px, yh * 2 + yl, pz].astype(F32)
        copy = pltpu.make_async_copy(value, out, sem.at[5 + n])
        copy.start()
        copies.append(copy)
    for copy in copies:
        copy.wait()


def on_device(
    byte_ids,
    global_out,
    global_in_grad,
    out_grad,
    proj_weight,
    emb_local,
    norm_gain,
    up_weight,
    down_weight,
):
    scratch = [pltpu.VMEM(shape, kind) for _, shape, kind in FIXED]
    scratch += [pltpu.VMEM(shape, BF) for _, shape in TABLE] * 2
    for _, width, order in ALL_UNITS:
        scratch += unit_scratch(width, order)
    dma = pltpu.SemaphoreType.DMA
    for count in N_SEMS.values():
        scratch += [dma((count,)), dma((count,))]
    scratch += [dma((9, 15)), dma((9, 15))]
    vmem = pl.BlockSpec(memory_space=pltpu.VMEM)
    anywhere = pl.BlockSpec(memory_space=pl.ANY)
    parts = pl.pallas_call(
        kernel,
        out_shape=(
            pltpu.VMEM((8, 32, 1024), BF),
            pltpu.VMEM((2, 4, 4, 4, 16, 128), BF),
            pltpu.VMEM((2, 4, 4, 4, 16, 128), BF),
            pltpu.VMEM((1, 1024), F32),
            pltpu.VMEM((8, 1024), F32),
            pltpu.VMEM((16, 1024), F32),
            pltpu.VMEM((16, 1024), F32),
        ),
        in_specs=[vmem] + [anywhere] * 5 + [vmem] + [anywhere] * 2,
        out_specs=[vmem] * 7,
        scratch_shapes=scratch,
        compiler_params=pltpu.CompilerParams(
            collective_id=0, has_side_effects=True, vmem_limit_bytes=52 * 1024 * 1024
        ),
    )(
        byte_ids.T,
        global_out.reshape(8, 32, 1024),
        global_in_grad,
        out_grad,
        proj_weight,
        emb_local,
        norm_gain.reshape(1, 1024),
        up_weight,
        down_weight,
    )
    out = jax.ShapeDtypeStruct
    gog, embg, embl, gain, proj, up, down = pl.pallas_call(
        finish,
        out_shape=(
            out((8, 32, 1024), BF),
            out((256, 1024), F32),
            out((256, 1024), F32),
            out((1, 1024), F32),
            out((8, 1024), F32),
            out((16, 1024), F32),
            out((16, 1024), F32),
        ),
        in_specs=[vmem] * 7,
        out_specs=[anywhere] * 7,
        scratch_shapes=[pltpu.VMEM((256, 1024), F32), pltpu.VMEM((256, 1024), F32), dma((7,))],
        compiler_params=pltpu.CompilerParams(vmem_limit_bytes=6 * 1024 * 1024),
    )(*parts)
    return gog.reshape(256, 1024), embg, embl, gain.reshape(1024), proj.T, up.T, down


def solution(mesh):
    placed = (
        P("seq", None),
        P("seq", "tp"),
        P("seq", "tp"),
        P(("seq", "tp"), None),
        P(),
        P(),
        P(),
        P(),
        P(),
    )
    return jax.shard_map(
        on_device,
        mesh=mesh,
        in_specs=placed,
        out_specs=(
            P("seq", "tp"),
            P(),
            P(),
            P(),
            P(None, ("seq", "tp")),
            P(None, ("seq", "tp")),
            P(("seq", "tp"), None),
        ),
        check_vma=False,
    )
```

```python
import jax
import jax.numpy as jnp
from jax import lax
from jax.experimental import pallas as pl
from jax.experimental.pallas import tpu as pltpu
from jax.sharding import PartitionSpec as P

BF = jnp.bfloat16
F32 = jnp.float32
MESH = pl.DeviceIdType.MESH
ALL = slice(None)
D_UNITS = ((0, 256, (0, 1, 2)), (256, 384, (1, 2, 0)), (640, 384, (2, 0, 1)))
U_UNITS = ((0, 256, (0, 1, 2)), (256, 384, (1, 2, 0)), (640, 384, (2, 0, 1)))
P_UNITS = ((0, 256, (0, 1, 2)), (256, 128, (1, 2, 0)), (384, 128, (2, 0, 1)))
ALL_UNITS = D_UNITS + U_UNITS + P_UNITS
FAR_FIRST = (2, 1, 3)
PLANE = tuple((ky, kz) for ky in (2, 1, 3, 0) for kz in (2, 1, 3, 0) if ky or kz)


def mm(a, b):
    return lax.dot_general(a, b, (((1,), (0,)), ((), ())), preferred_element_type=F32)


def mm_nt(a, b):
    return lax.dot_general(a, b, (((1,), (1,)), ((), ())), preferred_element_type=F32)


def mm_tn(a, b):
    return lax.dot_general(a, b, (((0,), (0,)), ((), ())), preferred_element_type=F32)


def iota(shape, dim):
    return lax.broadcasted_iota(jnp.int32, shape, dim)


def remote(src, dst, send, recv, device):
    return pltpu.make_async_remote_copy(
        src_ref=src, dst_ref=dst, send_sem=send, recv_sem=recv, device_id=device, device_id_type=MESH
    )


def await_recv(ref, sem, device):
    remote(ref, ref, sem, sem, device).wait_recv()


def await_send(ref, sem, device):
    remote(ref, ref, sem, sem, device).wait_send()


class Ring:
    def __init__(self, src, cols, over, half, spot, device_at, buf, out, send, recv):
        self.src, self.cols, self.over, self.half = src, cols, over, half
        self.buf, self.out, self.send, self.recv = buf, out, send, recv
        here = spot[over]
        self.here, self.right, self.left, self.far = here, (here + 1) % 4, (here + 3) % 4, (here + 2) % 4
        self.to_right = device_at(over, self.right)
        self.to_left = device_at(over, self.left)

    def part(self, place, half):
        index = tuple(
            place if a == self.over else pl.ds(2 * half, 2) if a == self.half else ALL for a in (0, 1, 2)
        )
        return self.src.at[index + (ALL, pl.ds(*self.cols))]

    def start(self):
        for src, n, sem, device in (
            (self.part(self.far, 0), 0, 0, self.to_right),
            (self.part(self.far, 1), 1, 0, self.to_left),
            (self.part(self.right, 1), 2, 1, self.to_right),
            (self.part(self.left, 0), 3, 1, self.to_left),
        ):
            remote(src, self.buf.at[n], self.send, self.recv[sem], device).start()

    def relay(self):
        await_recv(self.buf.at[pl.ds(0, 2)], self.recv[0], self.to_left)
        self.buf[0] = (self.buf[0].astype(F32) + self.part(self.right, 0)[...].astype(F32)).astype(BF)
        remote(self.buf.at[0], self.buf.at[4], self.send, self.recv[1], self.to_right).start()
        self.buf[1] = (self.buf[1].astype(F32) + self.part(self.left, 1)[...].astype(F32)).astype(BF)
        remote(self.buf.at[1], self.buf.at[5], self.send, self.recv[1], self.to_left).start()

    def out_half(self, half):
        index = tuple(pl.ds(2 * half, 2) if a == self.half else ALL for a in (0, 1, 2) if a != self.over)
        return self.out.at[index]

    def finish(self):
        await_recv(self.buf.at[pl.ds(2, 4)], self.recv[1], self.to_left)
        for half in range(2):
            self.out_half(half)[...] = (
                self.part(self.here, half)[...].astype(F32)
                + self.buf[4 + half].astype(F32)
                + self.buf[3 - half].astype(F32)
            ).astype(BF)

    def drain(self):
        await_send(self.buf, self.send, self.to_left)


class Direct:
    def __init__(self, src, axes, over, spot, device_at, buf, send, recv):
        self.src, self.axes, self.over, self.buf, self.send, self.recv = src, axes, over, buf, send, recv
        self.here = spot[over]
        self.device_at = device_at

    def part(self, place):
        return self.src.at[tuple(place if a == self.over else ALL for a in self.axes)]

    def start(self):
        for k in FAR_FIRST:
            there = (self.here + k) % 4
            self.to = self.device_at(self.over, there)
            remote(self.part(there), self.buf.at[k - 1], self.send, self.recv, self.to).start()

    def finish(self):
        await_recv(self.buf, self.recv, self.to)
        total = self.part(self.here)[...].astype(F32)
        for k in range(3):
            total = total + self.buf[k].astype(F32)
        return total

    def drain(self):
        await_send(self.buf, self.send, self.to)


class Unit:
    def __init__(self, src, cols, order, spot, device_at, bufs, sems):
        a, b, c = order
        first, out1, second, self.out2, last = bufs
        rest = tuple(n for n in (0, 1, 2) if n != a)
        self.one = Ring(src, cols, a, b, spot, device_at, first, out1, sems.at[0], (sems.at[1], sems.at[2]))
        self.two = Direct(out1, rest, b, spot, device_at, second, sems.at[3], sems.at[4])
        self.three = Direct(self.out2, (c,), c, spot, device_at, last, sems.at[5], sems.at[6])

    def start2(self):
        self.one.finish()
        self.two.start()

    def start3(self):
        self.out2[...] = self.two.finish().astype(BF)
        self.three.start()

    def drain(self):
        self.one.drain()
        self.two.drain()
        self.three.drain()


class Table:
    def __init__(self, bufs, gathered, spot, core, device, device_at, partner, sems):
        src, self.one, recv1, self.recv2 = bufs
        self.partner, self.sems = partner, sems
        x, y, z = spot
        self.spot = spot
        self.first = Direct(src, (0, 1, 2), 0, spot, device_at, recv1, sems.at[0], sems.at[1])
        self.own = (gathered.at[core, x, y, z], gathered.at[core, x], gathered.at[core])
        self.sized = (self.recv2, recv1, gathered.at[core])
        self.plane = []
        for ky, kz in PLANE:
            py, pz = (y + ky) % 4, (z + kz) % 4
            self.plane.append((py, pz, ky * 4 + kz - 1, device(x, py, pz, core)))
        self.to = (
            [there for _, _, _, there in self.plane],
            [device_at(0, (x + k) % 4) for k in FAR_FIRST],
            [partner],
        )

    def start(self, step):
        send, recv = self.sems.at[2 * step], self.sems.at[2 * step + 1]
        if step == 0:
            self.first.start()
        elif step == 1:
            for py, pz, n, there in self.plane:
                remote(self.one.at[py, pz], self.recv2.at[n], send, recv, there).start()
        else:
            n = step - 2
            for there in self.to[n]:
                remote(self.own[n], self.own[n], send, recv, there).start()

    def finish(self, step):
        if step == 0:
            self.one[...] = self.first.finish().astype(BF)
            return
        await_recv(self.recv2 if step == 1 else self.sized[step - 2], self.sems.at[2 * step + 1], self.partner)
        if step == 1:
            total = self.one[self.spot[1], self.spot[2]].astype(F32)
            for n in range(15):
                total = total + self.recv2[n].astype(F32)
            self.own[0][...] = total.astype(BF)

    def drain(self):
        self.first.drain()
        await_send(self.recv2, self.sems.at[2], self.partner)
        for n in range(3):
            await_send(self.sized[n], self.sems.at[2 * n + 4], self.partner)


def unit_scratch(width, order):
    a, b, c = order
    rest = tuple(n for n in (0, 1, 2) if n != a)
    one = tuple(2 if n == b else 4 for n in rest)
    return [
        pltpu.VMEM((6,) + one + (16, width), BF),
        pltpu.VMEM((4, 4, 16, width), BF),
        pltpu.VMEM((3, 4, 16, width), BF),
        pltpu.VMEM((4, 16, width), BF),
        pltpu.VMEM((3, 16, width), BF),
    ]


FIXED = (
    ("ids", (8, 256), jnp.int32),
    ("gain", (1, 1024), F32),
    ("og", (256, 1024), BF),
    ("dn", (2048, 1024), BF),
    ("gig", (256, 1024), BF),
    ("pw", (1024, 1024), BF),
    ("emb", (256, 1024), BF),
    ("up", (1024, 2048), BF),
    ("og2", (512, 1024), BF),
    ("slot", (8, 32, 1024), BF),
    ("dh", (8, 256, 256), F32),
    ("norm", (256, 1024), F32),
    ("scale", (256, 128), F32),
    ("r2", (512, 1024), BF),
    ("hot", (256, 256), BF),
    ("ht", (2, 1024, 512), BF),
    ("dat", (2, 1024, 512), BF),
    ("da", (256, 2048), BF),
    ("dr", (256, 1024), F32),
    ("du", (256, 1024), BF),
    ("dut", (1024, 256), BF),
    ("dp", (4, 4, 4, 16, 1024), BF),
    ("upart", (4, 4, 4, 16, 1024), BF),
    ("pp", (2, 4, 4, 4, 16, 512), BF),
    ("pr", (4, 4, 4, 16, 512), BF),
    ("gog", (8, 32, 1024), BF),
    ("gp", (4, 4, 1, 1024), F32),
)
TABLE = (
    ("part", (2, 4, 4, 4, 16, 128)),
    ("src", (4, 4, 4, 16, 128)),
    ("one", (4, 4, 16, 128)),
    ("recv1", (3, 4, 4, 16, 128)),
    ("recv2", (15, 16, 128)),
)
N_LOADS, N_X = 10, 14


def kernel(*refs):
    ids_h, go_h, gig_h, og_h, pw_h, emb_h, gain_h, up_h, dn_h = refs[:9]
    gog_o, table_g, table_l, gain_o, proj_o, up_o, down_o = refs[9:16]
    rest = list(refs[16:])
    buf = {name: rest.pop(0) for name, _, _ in FIXED}
    eg = {name: rest.pop(0) for name, _ in TABLE}
    el = {name: rest.pop(0) for name, _ in TABLE}
    unit_bufs = []
    for _ in ALL_UNITS:
        unit_bufs.append([rest.pop(0) for _ in range(5)])
    load_sem, x_send, x_recv, ab_sem, g_sem, tg_sem, tl_sem, u_sem = rest
    ids, gain = buf["ids"], buf["gain"]
    og, dn, gig, pw, emb, up = (buf[n] for n in ("og", "dn", "gig", "pw", "emb", "up"))
    og2, slot, dh, norm, scale, r2 = (buf[n] for n in ("og2", "slot", "dh", "norm", "scale", "r2"))
    hot, ht, dat, da = (buf[n] for n in ("hot", "ht", "dat", "da"))
    dr, du, dut, dp, upart, pp = (buf[n] for n in ("dr", "du", "dut", "dp", "upart", "pp"))
    pr, gog, gp = (buf[n] for n in ("pr", "gog", "gp"))

    seq = lax.axis_index("seq")
    tp = lax.axis_index("tp")
    core = seq % 2
    other = 1 - core
    x = seq // 4
    y = (seq // 2) % 2 * 2 + tp % 2
    z = tp // 2
    spot = (x, y, z)

    def device(px, py, pz, pc):
        return ((px * 2 + py // 2) * 2 + pc, pz * 2 + py % 2)

    def device_at(axis, place):
        where = list(spot)
        where[axis] = place
        return device(*where, core)

    partner = device(x, y, z, other)

    barrier = pltpu.get_barrier_semaphore()
    pl.semaphore_signal(barrier, inc=1, device_id=partner, device_id_type=MESH)
    for ky, kz in PLANE:
        there = device(x, (y + ky) % 4, (z + kz) % 4, core)
        pl.semaphore_signal(barrier, inc=1, device_id=there, device_id_type=MESH)
    for k in FAR_FIRST:
        pl.semaphore_signal(barrier, inc=1, device_id=device_at(0, (x + k) % 4), device_id_type=MESH)
    loads = {}
    for n, group in enumerate(
        (
            (("og", og_h, og),),
            (("dn", dn_h, dn),),
            (("ids", ids_h, ids),),
            (("gig", gig_h, gig),),
            (("pw", pw_h, pw),),
            (("emb", emb_h, emb),),
            (("up", up_h, up),),
            (("own", go_h.at[tp], slot.at[tp]),),
            (("gain", gain_h, gain),),
        )
    ):
        for name, src, dst in group:
            loads[name] = pltpu.make_async_copy(src, dst, load_sem.at[n])
            loads[name].start()
    pl.semaphore_wait(barrier, 19)

    def to_group(src, dst, sem, offsets):
        for k in offsets:
            device = (seq, (tp + k) % 8)
            remote(src.at[(tp + k) % 8], dst.at[tp], ab_sem.at[sem], ab_sem.at[sem + 1], device).start()

    to_group(go_h, slot, 0, range(1, 8))

    def swap(n, src, dst):
        copy = remote(src, dst, x_send.at[n], x_recv.at[n], partner)
        copy.start()
        return copy

    loads["og"].wait()
    row, col = iota((256, 256), 0), iota((256, 256), 1)
    perm = (col == 8 * (row % 32) + row // 32).astype(BF)
    own, far = pl.ds(0, 256), pl.ds(256, 256)
    og2[own, :] = mm(perm, og[...]).astype(BF)
    x_og = swap(0, og2.at[own], og2.at[far])

    loads["dn"].wait()

    def dh_step(n, carry):
        at = pl.ds(pl.multiple_of(n * 256, 256), 256)
        dh[n] = mm_nt(og2[own, :], dn[at, :])
        return carry

    lax.fori_loop(0, 8, dh_step, 0)

    loads["ids"].wait()
    ids_v = ids[...]
    own_id = jnp.sum(jnp.where(iota((8, 256), 0) == tp, ids_v, 0), axis=0, keepdims=True)
    hot_own = (row == own_id).astype(BF)
    pick = (row == tp * 32 + col % 32).astype(BF)
    ids_here = mm(ids_v.astype(F32).astype(BF), pick)
    col8 = iota((8, 256), 1)
    prev = jnp.sum(jnp.where(iota((8, 256), 0) == col8 // 32 - 1, ids_here, 0.0), axis=0, keepdims=True)
    prev_id = jnp.where(iota((1, 256), 1) < 32, -1, prev.astype(jnp.int32))
    hot[...] = (row == prev_id).astype(BF)

    def table_of(bufs, gathered, sems):
        order = tuple(bufs[n] for n in ("src", "one", "recv1", "recv2"))
        return Table(order, gathered, spot, core, device, device_at, partner, sems)

    glob, loc = table_of(eg, table_g, tg_sem), table_of(el, table_l, tl_sem)

    def put_table(part, n, value):
        block = value.astype(BF).reshape(4, 2, 2, 16, 256)
        for c in range(2):
            for yh in range(2):
                for yl in range(2):
                    part[c, :, yh * 2 + yl, n] = block[:, yh, c, :, yl * 128 : yl * 128 + 128]

    def join(part, src):
        def step(i, carry):
            src[i] = (src[i].astype(F32) + part[core, i].astype(F32)).astype(BF)
            return carry

        lax.fori_loop(0, 4, step, 0)

    loads["gig"].wait()
    for n in range(4):
        put_table(eg["part"], n, mm(hot_own, gig[:, n * 256 : n * 256 + 256]))
    x_eg = swap(1, eg["part"].at[other], eg["src"])

    loads["pw"].wait()
    loads["emb"].wait()
    loads["own"].wait()
    loads["gain"].wait()
    x_eg.wait_recv()
    join(eg["part"], eg["src"])
    glob.start(0)
    seven = pl.ds(0, 7)
    await_recv(slot.at[seven], ab_sem.at[1], partner)

    square = jnp.zeros((256, 1), F32)
    slot_v = slot[...].reshape(256, 1024)
    for n in range(4):
        at = slice(n * 256, n * 256 + 256)
        u_part = mm(slot_v, pw[:, at]) + mm_tn(hot[...], emb[:, at])
        norm[:, at] = u_part
        square = square + jnp.sum(u_part * u_part, axis=1, keepdims=True)
    scale_v = lax.rsqrt(square * (1.0 / 1024.0) + 1e-05)
    scale[...] = jnp.broadcast_to(scale_v, (256, 128))
    for n in range(4):
        at = slice(n * 256, n * 256 + 256)
        normed = norm[:, at] * scale_v
        norm[:, at] = normed
        r2[own, at] = (normed * gain[:, at]).astype(BF)
    x_r = swap(2, r2.at[own], r2.at[far])

    loads["up"].wait()

    def h_swap(j):
        rows = pl.ds(pl.multiple_of(j * 256, 256), 256)
        return remote(
            ht.at[other, rows, own], ht.at[other, rows, far], x_send.at[6 + j], x_recv.at[6 + j], partner
        )

    def ff_step(j, carry):
        for k2 in range(2):
            k = j * 2 + k2
            at = pl.ds(pl.multiple_of(k * 256, 256), 256)
            rows = pl.ds(pl.multiple_of(k * 128, 128), 128)
            a = mm(r2[own, :], up[:, at])
            sig = jax.nn.sigmoid(a)
            h_t = (a * sig).astype(BF).T
            ht[0, rows, own] = h_t[:128]
            ht[1, rows, own] = h_t[128:]
            da_v = (dh[k] * sig * (1.0 + a * (1.0 - sig))).astype(BF)
            da[:, at] = da_v
            da_t = da_v.T
            dat[0, rows, own] = da_t[:128]
            dat[1, rows, own] = da_t[128:]
        h_swap(j).start()
        return carry

    lax.fori_loop(0, 4, ff_step, 0)
    glob.finish(0)
    glob.start(1)

    def units(src, table, first):
        return [
            Unit(src, t[:2], t[2], spot, device_at, unit_bufs[first + i], u_sem.at[first + i])
            for i, t in enumerate(table)
        ]

    d_units = units(dp, D_UNITS, 0)
    u_units = units(upart, U_UNITS, 3)
    p_units = units(pr, P_UNITS, 6)

    def big(lhs, rhs, out, n):
        at = slice(n * 256, n * 256 + 256)

        def step(g, carry):
            rows = pl.ds(pl.multiple_of(g * 512, 512), 512)
            v = mm(lhs[core, rows, :], rhs[:, at]).astype(BF).reshape(2, 2, 4, 2, 16, 256)
            for xx in range(2):
                for yh in range(2):
                    for yl in range(2):
                        out[2 * g + xx, yh * 2 + yl, :, :, at] = v[xx, yh, :, yl]
            return carry

        lax.fori_loop(0, 2, step, 0)

    for n in range(4):
        at = slice(n * 256, n * 256 + 256)
        dr[:, at] = mm_nt(da[...], up[at, :])
    x_og.wait_recv()
    for j in range(4):
        h_swap(j).wait_recv()
    x_da = swap(4, dat.at[other, :, own], dat.at[other, :, far])
    big(ht, og2, dp, 0)
    d_units[0].one.start()
    big(ht, og2, dp, 1)
    big(ht, og2, dp, 2)
    d_units[1].one.start()
    big(ht, og2, dp, 3)
    d_units[2].one.start()
    glob.finish(1)
    glob.start(2)
    x_r.wait_recv()
    x_da.wait_recv()
    big(dat, r2, upart, 0)
    u_units[0].one.start()
    big(dat, r2, upart, 1)
    big(dat, r2, upart, 2)
    u_units[1].one.start()
    big(dat, r2, upart, 3)
    u_units[2].one.start()
    gain_v = gain[...]

    def du_step(i, total):
        rows = pl.ds(pl.multiple_of(i * 32, 32), 32)
        dr_v = dr[rows, :]
        normed = norm[rows, :]
        product = dr_v * normed
        dn_v = dr_v * gain_v
        mean = jnp.sum(product * gain_v, axis=1, keepdims=True) * (1.0 / 1024.0)
        du_v = og2[rows, :].astype(F32) + scale[rows, 0:1] * (dn_v - normed * mean)
        du[rows, :] = du_v.astype(BF)
        return total + jnp.sum(product.reshape(4, 8, 1024), axis=0)

    gain_part = lax.fori_loop(0, 8, du_step, jnp.zeros((8, 1024), F32))
    for n in range(4):
        put_table(el["part"], n, mm(hot[...], du[:, n * 256 : n * 256 + 256]))
    x_el = swap(3, el["part"].at[other], el["src"])
    gp[0, core] = jnp.sum(gain_part, axis=0, keepdims=True)
    x_g = swap(5, gp.at[0, core], gp.at[0, core])
    for unit in d_units:
        unit.one.relay()
    for n in range(4):
        at = slice(n * 256, n * 256 + 256)
        dut[at, :] = du[:, at].T

    def gain_swap(step):
        axis = step - 1
        mine = gp.at[step, spot[axis]]
        for k in FAR_FIRST:
            device = device_at(axis, (spot[axis] + k) % 4)
            remote(mine, mine, g_sem.at[2 * axis], g_sem.at[2 * axis + 1], device).start()

    def gain_join(step):
        three = gp.at[step, pl.ds(0, 3)]
        await_recv(three, g_sem.at[2 * step - 1], partner)
        await_send(three, g_sem.at[2 * step - 2], partner)
        return gp[step, 0] + gp[step, 1] + gp[step, 2] + gp[step, 3]

    def p_swap(g):
        return remote(pp.at[other, g], pr.at[g], x_send.at[10 + g], x_recv.at[10 + g], partner)

    def proj_step(g, carry):
        rows = pl.ds(pl.multiple_of(g * 256, 256), 256)
        for n in range(2):
            lo, hi = slice(n * 256, n * 256 + 256), slice(512 + n * 256, 768 + n * 256)
            v_lo = mm(dut[rows, :], slot[:, :, lo].reshape(256, 256)).reshape(2, 2, 4, 2, 8, 256)
            v_hi = mm(dut[rows, :], slot[:, :, hi].reshape(256, 256)).reshape(2, 2, 4, 2, 8, 256)
            v = jnp.concatenate([v_lo, v_hi], axis=4).astype(BF)
            for c in range(2):
                for yh in range(2):
                    for yl in range(2):
                        pp[c, g, yh * 2 + yl, :, :, lo] = v[yh, c, :, yl]
        p_swap(g).start()
        return carry

    lax.fori_loop(0, 4, proj_step, 0)
    x_el.wait_recv()
    join(el["part"], el["src"])
    loc.start(0)
    x_g.wait_recv()
    x_g.wait_send()
    gp[1, x] = gp[0, 0] + gp[0, 1]
    gain_swap(1)
    for n in range(4):
        at = slice(n * 256, n * 256 + 256)
        gog[:, :, at] = mm_nt(du[...], pw[at, :]).astype(BF).reshape(8, 32, 256)
    own_back = pltpu.make_async_copy(gog.at[tp], gog_o.at[tp], load_sem.at[9])
    own_back.start()
    for g in range(4):
        p_swap(g).wait_recv()
    join(pp, pr)
    for unit in p_units:
        unit.one.start()
    for unit in u_units:
        unit.one.relay()
    glob.finish(2)
    glob.start(3)
    loc.finish(0)
    loc.start(1)
    for unit in p_units:
        unit.one.relay()
    for unit in d_units:
        unit.start2()
    gp[2, y] = gain_join(1)
    gain_swap(2)
    loc.finish(1)
    loc.start(2)
    for unit in u_units:
        unit.start2()
    for unit in p_units:
        unit.start2()
    for unit in d_units:
        unit.start3()
    loc.finish(2)
    loc.start(3)
    to_group(gog, gog_o, 2, (1, 2, 3))
    gp[3, z] = gain_join(2)
    gain_swap(3)
    for unit in u_units:
        unit.start3()
    for unit in p_units:
        unit.start3()
    to_group(gog, gog_o, 2, (4, 5, 6, 7))
    glob.finish(3)
    glob.start(4)
    for i, unit in enumerate(d_units):
        down_o[:, pl.ds(*D_UNITS[i][:2])] = unit.three.finish()
    gain_o[...] = gain_join(3)
    loc.finish(3)
    loc.start(4)
    for i, unit in enumerate(u_units):
        up_o[:, pl.ds(*U_UNITS[i][:2])] = unit.three.finish()
    for i, unit in enumerate(p_units):
        first, width, _ = P_UNITS[i]
        value = unit.three.finish()
        proj_o[:, pl.ds(first, width)] = value[:8]
        proj_o[:, pl.ds(512 + first, width)] = value[8:]
    glob.finish(4)
    glob.drain()
    for unit in d_units + u_units + p_units:
        unit.drain()
    await_send(slot.at[seven], ab_sem.at[0], partner)
    for copy in (x_og, x_eg, x_r, x_da, x_el):
        copy.wait_send()
    for i in range(4):
        h_swap(i).wait_send()
        p_swap(i).wait_send()
    await_recv(gog_o.at[seven], ab_sem.at[3], partner)
    own_back.wait()
    await_send(gog_o.at[seven], ab_sem.at[2], partner)
    loc.finish(4)
    loc.drain()


def finish(gog, table_g, table_l, gain, proj, up, down, gog_o, embg_o, embl_o, gain_o, proj_o, up_o, down_o, embg, embl, sem):
    pairs = ((gog, gog_o), (gain, gain_o), (proj, proj_o), (up, up_o), (down, down_o))
    copies = [pltpu.make_async_copy(src, dst, sem.at[n]) for n, (src, dst) in enumerate(pairs)]
    for copy in copies:
        copy.start()
    for n, (table, value, out) in enumerate(((table_g, embg, embg_o), (table_l, embl, embl_o))):
        for row in range(16):
            px, yh, c = row // 4, row // 2 % 2, row % 2
            for col in range(8):
                pz, yl = col // 2, col % 2
                value[row * 16 : row * 16 + 16, col * 128 : col * 128 + 128] = table[c, px, yh * 2 + yl, pz].astype(F32)
        copy = pltpu.make_async_copy(value, out, sem.at[5 + n])
        copy.start()
        copies.append(copy)
    for copy in copies:
        copy.wait()


def on_device(
    byte_ids,
    global_out,
    global_in_grad,
    out_grad,
    proj_weight,
    emb_local,
    norm_gain,
    up_weight,
    down_weight,
):
    scratch = [pltpu.VMEM(shape, kind) for _, shape, kind in FIXED]
    scratch += [pltpu.VMEM(shape, BF) for _, shape in TABLE] * 2
    for _, width, order in ALL_UNITS:
        scratch += unit_scratch(width, order)
    dma = pltpu.SemaphoreType.DMA
    scratch += [dma((n,)) for n in (N_LOADS, N_X, N_X, 4, 6, 10, 10)] + [dma((len(ALL_UNITS), 7))]
    vmem = pl.BlockSpec(memory_space=pltpu.VMEM)
    anywhere = pl.BlockSpec(memory_space=pl.ANY)
    parts = pl.pallas_call(
        kernel,
        out_shape=(
            pltpu.VMEM((8, 32, 1024), BF),
            pltpu.VMEM((2, 4, 4, 4, 16, 128), BF),
            pltpu.VMEM((2, 4, 4, 4, 16, 128), BF),
            pltpu.VMEM((1, 1024), F32),
            pltpu.VMEM((8, 1024), F32),
            pltpu.VMEM((16, 1024), F32),
            pltpu.VMEM((16, 1024), F32),
        ),
        in_specs=[pl.BlockSpec(memory_space=pltpu.HBM)] * 9,
        out_specs=[vmem] * 7,
        scratch_shapes=scratch,
        compiler_params=pltpu.CompilerParams(
            collective_id=0, has_side_effects=True, vmem_limit_bytes=52 * 1024 * 1024
        ),
    )(
        pltpu.with_memory_space_constraint(byte_ids.T, pltpu.HBM),
        global_out.reshape(8, 32, 1024),
        global_in_grad,
        out_grad,
        proj_weight,
        emb_local,
        pltpu.with_memory_space_constraint(norm_gain.reshape(1, 1024), pltpu.HBM),
        up_weight,
        down_weight,
    )
    out = jax.ShapeDtypeStruct
    gog, embg, embl, gain, proj, up, down = pl.pallas_call(
        finish,
        out_shape=(
            out((8, 32, 1024), BF),
            out((256, 1024), F32),
            out((256, 1024), F32),
            out((1, 1024), F32),
            out((8, 1024), F32),
            out((16, 1024), F32),
            out((16, 1024), F32),
        ),
        in_specs=[vmem] * 7,
        out_specs=[anywhere] * 7,
        scratch_shapes=[pltpu.VMEM((256, 1024), F32), pltpu.VMEM((256, 1024), F32), dma((7,))],
        compiler_params=pltpu.CompilerParams(vmem_limit_bytes=6 * 1024 * 1024),
    )(*parts)
    return gog.reshape(256, 1024), embg, embl, gain.reshape(1024), proj.T, up.T, down


def solution(mesh):
    placed = (
        P("seq", None),
        P("seq", "tp"),
        P("seq", "tp"),
        P(("seq", "tp"), None),
        P(),
        P(),
        P(),
        P(),
        P(),
    )
    return jax.shard_map(
        on_device,
        mesh=mesh,
        in_specs=placed,
        out_specs=(
            P("seq", "tp"),
            P(),
            P(),
            P(),
            P(None, ("seq", "tp")),
            P(None, ("seq", "tp")),
            P(("seq", "tp"), None),
        ),
        check_vma=False,
    )
```

```python
import jax
import jax.numpy as jnp
from jax import lax
from jax.experimental import pallas as pl
from jax.experimental.pallas import tpu as pltpu
from jax.sharding import PartitionSpec as P

BF = jnp.bfloat16
F32 = jnp.float32
MESH = pl.DeviceIdType.MESH
ALL = slice(None)
D_UNITS = ((0, 256, (1, 2, 0)), (256, 384, (2, 0, 1)), (640, 384, (0, 1, 2)))
U_UNITS = ((0, 256, (0, 1, 2)), (256, 384, (1, 2, 0)), (640, 384, (2, 0, 1)))
P_UNITS = ((0, 128, (0, 1, 2)), (128, 256, (1, 2, 0)), (384, 128, (2, 0, 1)))
ALL_UNITS = D_UNITS + U_UNITS + P_UNITS
FAR_FIRST = (2, 1, 3)
PLANE = tuple((ky, kz) for ky in (2, 1, 3, 0) for kz in (2, 1, 3, 0) if ky or kz)


def mm(a, b):
    return lax.dot_general(a, b, (((1,), (0,)), ((), ())), preferred_element_type=F32)


def mm_nt(a, b):
    return lax.dot_general(a, b, (((1,), (1,)), ((), ())), preferred_element_type=F32)


def mm_tn(a, b):
    return lax.dot_general(a, b, (((0,), (0,)), ((), ())), preferred_element_type=F32)


def iota(shape, dim):
    return lax.broadcasted_iota(jnp.int32, shape, dim)


def remote(src, dst, send, recv, device):
    return pltpu.make_async_remote_copy(
        src_ref=src, dst_ref=dst, send_sem=send, recv_sem=recv, device_id=device, device_id_type=MESH
    )


def await_recv(ref, sem, device):
    remote(ref, ref, sem, sem, device).wait_recv()


def await_send(ref, sem, device):
    remote(ref, ref, sem, sem, device).wait_send()


class Ring:
    def __init__(self, src, cols, over, half, spot, device_at, buf, out, send, recv):
        self.src, self.cols, self.over, self.half = src, cols, over, half
        self.buf, self.out, self.send, self.recv = buf, out, send, recv
        here = spot[over]
        self.here, self.right, self.left, self.far = here, (here + 1) % 4, (here + 3) % 4, (here + 2) % 4
        self.to_right = device_at(over, self.right)
        self.to_left = device_at(over, self.left)

    def part(self, place, half):
        index = tuple(
            place if a == self.over else pl.ds(2 * half, 2) if a == self.half else ALL for a in (0, 1, 2)
        )
        return self.src.at[index + (ALL, pl.ds(*self.cols))]

    def start(self):
        for src, n, sem, device in (
            (self.part(self.far, 0), 0, 0, self.to_right),
            (self.part(self.far, 1), 1, 0, self.to_left),
            (self.part(self.right, 1), 2, 1, self.to_right),
            (self.part(self.left, 0), 3, 1, self.to_left),
        ):
            remote(src, self.buf.at[n], self.send, self.recv[sem], device).start()

    def relay(self):
        await_recv(self.buf.at[pl.ds(0, 2)], self.recv[0], self.to_left)
        self.buf[0] = (self.buf[0].astype(F32) + self.part(self.right, 0)[...].astype(F32)).astype(BF)
        remote(self.buf.at[0], self.buf.at[4], self.send, self.recv[1], self.to_right).start()
        self.buf[1] = (self.buf[1].astype(F32) + self.part(self.left, 1)[...].astype(F32)).astype(BF)
        remote(self.buf.at[1], self.buf.at[5], self.send, self.recv[1], self.to_left).start()

    def out_half(self, half):
        index = tuple(pl.ds(2 * half, 2) if a == self.half else ALL for a in (0, 1, 2) if a != self.over)
        return self.out.at[index]

    def finish(self):
        await_recv(self.buf.at[pl.ds(2, 4)], self.recv[1], self.to_left)
        for half in range(2):
            self.out_half(half)[...] = (
                self.part(self.here, half)[...].astype(F32)
                + self.buf[4 + half].astype(F32)
                + self.buf[3 - half].astype(F32)
            ).astype(BF)

    def drain(self):
        await_send(self.buf, self.send, self.to_left)


class Direct:
    def __init__(self, src, axes, over, spot, device_at, buf, send, recv):
        self.src, self.axes, self.over, self.buf, self.send, self.recv = src, axes, over, buf, send, recv
        self.here = spot[over]
        self.device_at = device_at

    def part(self, place):
        return self.src.at[tuple(place if a == self.over else ALL for a in self.axes)]

    def start(self):
        for k in FAR_FIRST:
            there = (self.here + k) % 4
            self.to = self.device_at(self.over, there)
            remote(self.part(there), self.buf.at[k - 1], self.send, self.recv, self.to).start()

    def finish(self):
        await_recv(self.buf, self.recv, self.to)
        total = self.part(self.here)[...].astype(F32)
        for k in range(3):
            total = total + self.buf[k].astype(F32)
        return total

    def drain(self):
        await_send(self.buf, self.send, self.to)


class Unit:
    def __init__(self, src, cols, order, spot, device_at, bufs, sems):
        a, b, c = order
        first, out1, second, self.out2, last = bufs
        rest = tuple(n for n in (0, 1, 2) if n != a)
        self.one = Ring(src, cols, a, b, spot, device_at, first, out1, sems.at[0], (sems.at[1], sems.at[2]))
        self.two = Direct(out1, rest, b, spot, device_at, second, sems.at[3], sems.at[4])
        self.three = Direct(self.out2, (c,), c, spot, device_at, last, sems.at[5], sems.at[6])

    def start2(self):
        self.one.finish()
        self.two.start()

    def start3(self):
        self.out2[...] = self.two.finish().astype(BF)
        self.three.start()

    def drain(self):
        self.one.drain()
        self.two.drain()
        self.three.drain()


class Table:
    def __init__(self, bufs, gathered, spot, core, device, device_at, partner, sems):
        src, self.one, recv1, self.recv2 = bufs
        self.partner, self.sems = partner, sems
        x, y, z = spot
        self.spot = spot
        self.first = Direct(src, (0, 1, 2), 0, spot, device_at, recv1, sems.at[0], sems.at[1])
        self.own = (gathered.at[core, x, y, z], gathered.at[core, x], gathered.at[core])
        self.sized = (self.recv2, recv1, gathered.at[core])
        self.plane = []
        for ky, kz in PLANE:
            py, pz = (y + ky) % 4, (z + kz) % 4
            self.plane.append((py, pz, ky * 4 + kz - 1, device(x, py, pz, core)))
        self.to = (
            [there for _, _, _, there in self.plane],
            [device_at(0, (x + k) % 4) for k in FAR_FIRST],
            [partner],
        )

    def start(self, step):
        send, recv = self.sems.at[2 * step], self.sems.at[2 * step + 1]
        if step == 0:
            self.first.start()
        elif step == 1:
            for py, pz, n, there in self.plane:
                remote(self.one.at[py, pz], self.recv2.at[n], send, recv, there).start()
        else:
            n = step - 2
            for there in self.to[n]:
                remote(self.own[n], self.own[n], send, recv, there).start()

    def finish(self, step):
        if step == 0:
            self.one[...] = self.first.finish().astype(BF)
            return
        await_recv(self.recv2 if step == 1 else self.sized[step - 2], self.sems.at[2 * step + 1], self.partner)
        if step == 1:
            total = self.one[self.spot[1], self.spot[2]].astype(F32)
            for n in range(15):
                total = total + self.recv2[n].astype(F32)
            self.own[0][...] = total.astype(BF)

    def drain(self):
        self.first.drain()
        await_send(self.recv2, self.sems.at[2], self.partner)
        for n in range(3):
            await_send(self.sized[n], self.sems.at[2 * n + 4], self.partner)


def unit_scratch(width, order):
    a, b, c = order
    rest = tuple(n for n in (0, 1, 2) if n != a)
    one = tuple(2 if n == b else 4 for n in rest)
    return [
        pltpu.VMEM((6,) + one + (16, width), BF),
        pltpu.VMEM((4, 4, 16, width), BF),
        pltpu.VMEM((3, 4, 16, width), BF),
        pltpu.VMEM((4, 16, width), BF),
        pltpu.VMEM((3, 16, width), BF),
    ]


FIXED = (
    ("ids", (8, 256), jnp.int32),
    ("gain", (1, 1024), F32),
    ("og", (256, 1024), BF),
    ("dn", (2048, 1024), BF),
    ("gig", (256, 1024), BF),
    ("pw", (1024, 1024), BF),
    ("emb", (256, 1024), BF),
    ("up", (1024, 2048), BF),
    ("ogp", (8, 2, 16, 1024), BF),
    ("og2", (2, 8, 2, 16, 1024), BF),
    ("slot", (256, 1024), BF),
    ("slope", (8, 256, 256), F32),
    ("norm", (256, 1024), F32),
    ("scale", (256, 128), F32),
    ("r2", (512, 1024), BF),
    ("hot", (256, 256), BF),
    ("ht", (2, 1024, 512), BF),
    ("dat", (2, 1024, 512), BF),
    ("da", (256, 2048), BF),
    ("dr", (256, 1024), F32),
    ("du", (256, 1024), BF),
    ("dut", (1024, 256), BF),
    ("dp", (4, 4, 4, 16, 1024), BF),
    ("upart", (4, 4, 4, 16, 1024), BF),
    ("pp", (2, 4, 4, 4, 16, 512), BF),
    ("pr", (4, 4, 4, 16, 512), BF),
    ("gp", (4, 4, 1, 1024), F32),
)
TABLE = (
    ("part", (2, 4, 4, 4, 16, 128)),
    ("src", (4, 4, 4, 16, 128)),
    ("one", (4, 4, 16, 128)),
    ("recv1", (3, 4, 4, 16, 128)),
    ("recv2", (15, 16, 128)),
)
N_LOADS, N_X = 10, 18


def kernel(*refs):
    ids_h, go_h, gig_h, og_h, pw_h, emb_h, gain_h, up_h, dn_h = refs[:9]
    gog_o, table_g, table_l, gain_o, proj_o, up_o, down_o = refs[9:16]
    rest = list(refs[16:])
    buf = {name: rest.pop(0) for name, _, _ in FIXED}
    eg = {name: rest.pop(0) for name, _ in TABLE}
    el = {name: rest.pop(0) for name, _ in TABLE}
    unit_bufs = []
    for _ in ALL_UNITS:
        unit_bufs.append([rest.pop(0) for _ in range(5)])
    load_sem, x_send, x_recv, ab_sem, g_sem, tg_sem, tl_sem, u_sem = rest
    ids, gain = buf["ids"], buf["gain"]
    og, dn, gig, pw, emb, up = (buf[n] for n in ("og", "dn", "gig", "pw", "emb", "up"))
    og2, slot, slope, norm, scale, r2 = (buf[n] for n in ("og2", "slot", "slope", "norm", "scale", "r2"))
    hot, ht, dat, da = (buf[n] for n in ("hot", "ht", "dat", "da"))
    dr, du, dut, dp, upart, pp = (buf[n] for n in ("dr", "du", "dut", "dp", "upart", "pp"))
    pr, gp, ogp = (buf[n] for n in ("pr", "gp", "ogp"))

    seq = lax.axis_index("seq")
    tp = lax.axis_index("tp")
    core = seq % 2
    other = 1 - core
    x = seq // 4
    y = (seq // 2) % 2 * 2 + tp % 2
    z = tp // 2
    spot = (x, y, z)

    def device(px, py, pz, pc):
        return ((px * 2 + py // 2) * 2 + pc, pz * 2 + py % 2)

    def device_at(axis, place):
        where = list(spot)
        where[axis] = place
        return device(*where, core)

    partner = device(x, y, z, other)

    barrier = pltpu.get_barrier_semaphore()
    pl.semaphore_signal(barrier, inc=1, device_id=partner, device_id_type=MESH)
    for ky, kz in PLANE:
        there = device(x, (y + ky) % 4, (z + kz) % 4, core)
        pl.semaphore_signal(barrier, inc=1, device_id=there, device_id_type=MESH)
    for k in FAR_FIRST:
        pl.semaphore_signal(barrier, inc=1, device_id=device_at(0, (x + k) % 4), device_id_type=MESH)
    loads = {}
    for n, group in enumerate(
        (
            (("og", og_h, og),),
            (("slot", go_h, slot),),
            (("pw", pw_h, pw),),
            (("ids", ids_h, ids),),
            (("emb", emb_h, emb),),
            (("gain", gain_h, gain),),
            (("gig", gig_h, gig),),
            (("up", up_h, up),),
            (("dn", dn_h, dn),),
        )
    ):
        for name, src, dst in group:
            loads[name] = pltpu.make_async_copy(src, dst, load_sem.at[n])
            loads[name].start()

    loads["og"].wait()
    row, col = iota((256, 256), 0), iota((256, 256), 1)
    own, far = pl.ds(0, 256), pl.ds(256, 256)
    perm = (col == 8 * (row % 32) + row // 32).astype(BF)
    ogp[...] = mm(perm, og[...]).astype(BF).reshape(8, 2, 16, 1024)
    keep = pltpu.make_async_copy(ogp.at[tp], og2.at[0, tp], load_sem.at[9])
    keep.start()
    pl.semaphore_wait(barrier, 19)
    for half in range(2):
        for k in range(1, 8):
            there = (tp + k) % 8
            remote(
                ogp.at[there, half], og2.at[0, tp, half], ab_sem.at[0], ab_sem.at[1 + half], (seq, there)
            ).start()

    def swap(n, src, dst):
        copy = remote(src, dst, x_send.at[n], x_recv.at[n], partner)
        copy.start()
        return copy

    loads["ids"].wait()
    ids_v = ids[...]
    row8 = iota((8, 256), 0)
    own_id = jnp.sum(jnp.where(row8 == tp, ids_v, 0), axis=0, keepdims=True)
    hot_own = (row == own_id).astype(BF)
    prev_id = jnp.sum(jnp.where(row8 == tp - 1, ids_v, 0), axis=0, keepdims=True) - (tp == 0).astype(jnp.int32)
    hot[...] = (row == prev_id).astype(BF)

    def table_of(bufs, gathered, sems):
        order = tuple(bufs[n] for n in ("src", "one", "recv1", "recv2"))
        return Table(order, gathered, spot, core, device, device_at, partner, sems)

    glob, loc = table_of(eg, table_g, tg_sem), table_of(el, table_l, tl_sem)

    def put_table(part, n, value):
        block = value.astype(BF).reshape(4, 2, 2, 16, 256)
        for c in range(2):
            for yh in range(2):
                for yl in range(2):
                    part[c, :, yh * 2 + yl, n] = block[:, yh, c, :, yl * 128 : yl * 128 + 128]

    def join(part, src):
        def step(i, carry):
            src[i] = (src[i].astype(F32) + part[core, i].astype(F32)).astype(BF)
            return carry

        lax.fori_loop(0, 4, step, 0)

    loads["gig"].wait()
    for n in range(4):
        put_table(eg["part"], n, mm(hot_own, gig[:, n * 256 : n * 256 + 256]))
    x_eg = swap(1, eg["part"].at[other], eg["src"])

    loads["pw"].wait()
    loads["emb"].wait()
    loads["slot"].wait()
    loads["gain"].wait()
    square = jnp.zeros((256, 1), F32)
    for n in range(4):
        at = slice(n * 256, n * 256 + 256)
        u_part = mm(slot[...], pw[:, at]) + mm_tn(hot[...], emb[:, at])
        norm[:, at] = u_part
        square = square + jnp.sum(u_part * u_part, axis=1, keepdims=True)
    scale_v = lax.rsqrt(square * (1.0 / 1024.0) + 1e-05)
    scale[...] = jnp.broadcast_to(scale_v, (256, 128))
    for n in range(4):
        at = slice(n * 256, n * 256 + 256)
        normed = norm[:, at] * scale_v
        norm[:, at] = normed
        r2[own, at] = (normed * gain[:, at]).astype(BF)
    x_r = swap(2, r2.at[own], r2.at[far])
    x_eg.wait_recv()
    join(eg["part"], eg["src"])
    glob.start(0)

    def t_swap(ref, base, j):
        rows = pl.ds(pl.multiple_of(j * 256, 256), 256)
        return remote(
            ref.at[other, rows, own], ref.at[other, rows, far], x_send.at[base + j], x_recv.at[base + j], partner
        )

    loads["up"].wait()

    def ff_step(j, carry):
        for k2 in range(2):
            k = j * 2 + k2
            at = pl.ds(pl.multiple_of(k * 256, 256), 256)
            rows = pl.ds(pl.multiple_of(k * 128, 128), 128)
            a = mm(r2[own, :], up[:, at])
            sig = jax.nn.sigmoid(a)
            h_t = (a * sig).astype(BF).T
            ht[0, rows, own] = h_t[:128]
            ht[1, rows, own] = h_t[128:]
            slope[k] = sig * (1.0 + a * (1.0 - sig))
        t_swap(ht, 6, j).start()
        return carry

    lax.fori_loop(0, 4, ff_step, 0)

    def da_step(j, carry):
        for k2 in range(2):
            k = j * 2 + k2
            at = pl.ds(pl.multiple_of(k * 256, 256), 256)
            rows = pl.ds(pl.multiple_of(k * 128, 128), 128)
            da_v = (mm_nt(og2[0].reshape(256, 1024), dn[at, :]) * slope[k]).astype(BF)
            da[:, at] = da_v
            da_t = da_v.T
            dat[0, rows, own] = da_t[:128]
            dat[1, rows, own] = da_t[128:]
        t_swap(dat, 10, j).start()
        return carry

    loads["dn"].wait()
    keep.wait()
    seven = pl.ds(0, 7)
    x_og = []
    for half in range(2):
        await_recv(og2.at[0, seven, half], ab_sem.at[1 + half], partner)
        x_og.append(swap((0, 4)[half], og2.at[0, :, half], og2.at[1, :, half]))
    lax.fori_loop(0, 2, da_step, 0)

    def units(src, table, first):
        return [
            Unit(src, t[:2], t[2], spot, device_at, unit_bufs[first + i], u_sem.at[first + i])
            for i, t in enumerate(table)
        ]

    d_units = units(dp, D_UNITS, 0)
    u_units = units(upart, U_UNITS, 3)
    p_units = units(pr, P_UNITS, 6)

    def big(lhs, rhs, out, n):
        at = slice(n * 256, n * 256 + 256)

        def step(g):
            rows = pl.ds(g * 512, 512)
            v = mm(lhs[core, rows, :], rhs(at)).astype(BF).reshape(2, 2, 4, 2, 16, 256)
            for xx in range(2):
                for yh in range(2):
                    for yl in range(2):
                        out[2 * g + xx, yh * 2 + yl, :, :, at] = v[xx, yh, :, yl]

        step(0)
        step(1)

    for j in range(4):
        t_swap(ht, 6, j).wait_recv()
    for copy in x_og:
        copy.wait_recv()

    def both_og(at):
        return og2[:, :, :, :, at].reshape(512, 256)

    def both_r(at):
        return r2[:, at]

    big(ht, both_og, dp, 0)
    d_units[0].one.start()
    big(ht, both_og, dp, 1)
    big(ht, both_og, dp, 2)
    d_units[1].one.start()
    big(ht, both_og, dp, 3)
    d_units[2].one.start()
    glob.finish(0)
    glob.start(1)
    lax.fori_loop(2, 4, da_step, 0)
    for n in range(4):
        at = slice(n * 256, n * 256 + 256)
        dr[:, at] = mm_nt(da[...], up[at, :])
    gain_v = gain[...]

    def du_step(i, total):
        rows = pl.ds(pl.multiple_of(i * 32, 32), 32)
        dr_v = dr[rows, :]
        normed = norm[rows, :]
        product = dr_v * normed
        dn_v = dr_v * gain_v
        mean = jnp.sum(product * gain_v, axis=1, keepdims=True) * (1.0 / 1024.0)
        du_v = og2[0, i].reshape(32, 1024).astype(F32) + scale[rows, 0:1] * (dn_v - normed * mean)
        du[rows, :] = du_v.astype(BF)
        return total + jnp.sum(product.reshape(4, 8, 1024), axis=0)

    gain_part = lax.fori_loop(0, 8, du_step, jnp.zeros((8, 1024), F32))
    for n in range(4):
        put_table(el["part"], n, mm(hot[...], du[:, n * 256 : n * 256 + 256]))
    x_el = swap(3, el["part"].at[other], el["src"])
    gp[0, core] = jnp.sum(gain_part, axis=0, keepdims=True)
    x_g = swap(5, gp.at[0, core], gp.at[0, core])
    for unit in d_units:
        unit.one.relay()
    x_el.wait_recv()
    join(el["part"], el["src"])
    loc.start(0)
    x_r.wait_recv()
    for j in range(4):
        t_swap(dat, 10, j).wait_recv()
    big(dat, both_r, upart, 0)
    u_units[0].one.start()
    big(dat, both_r, upart, 1)
    big(dat, both_r, upart, 2)
    u_units[1].one.start()
    big(dat, both_r, upart, 3)
    u_units[2].one.start()
    glob.finish(1)
    glob.start(2)
    for n in range(4):
        at = slice(n * 256, n * 256 + 256)
        dut[at, :] = du[:, at].T

    def gain_swap(step):
        axis = step - 1
        mine = gp.at[step, spot[axis]]
        for k in FAR_FIRST:
            device = device_at(axis, (spot[axis] + k) % 4)
            remote(mine, mine, g_sem.at[2 * axis], g_sem.at[2 * axis + 1], device).start()

    def gain_join(step):
        three = gp.at[step, pl.ds(0, 3)]
        await_recv(three, g_sem.at[2 * step - 1], partner)
        await_send(three, g_sem.at[2 * step - 2], partner)
        return gp[step, 0] + gp[step, 1] + gp[step, 2] + gp[step, 3]

    def p_swap(g):
        return remote(pp.at[other, g], pr.at[g], x_send.at[14 + g], x_recv.at[14 + g], partner)

    def proj_step(g, carry):
        rows = pl.ds(pl.multiple_of(g * 256, 256), 256)
        for n in range(2):
            lo, hi = slice(n * 256, n * 256 + 256), slice(512 + n * 256, 768 + n * 256)
            v_lo = mm(dut[rows, :], slot[:, lo]).reshape(2, 2, 4, 2, 8, 256)
            v_hi = mm(dut[rows, :], slot[:, hi]).reshape(2, 2, 4, 2, 8, 256)
            v = jnp.concatenate([v_lo, v_hi], axis=4).astype(BF)
            for c in range(2):
                for yh in range(2):
                    for yl in range(2):
                        pp[c, g, yh * 2 + yl, :, :, lo] = v[yh, c, :, yl]
        p_swap(g).start()
        return carry

    lax.fori_loop(0, 4, proj_step, 0)
    x_g.wait_recv()
    x_g.wait_send()
    gp[1, x] = gp[0, 0] + gp[0, 1]
    gain_swap(1)
    for n in range(4):
        at = slice(n * 256, n * 256 + 256)
        gog_o[:, at] = mm_nt(du[...], pw[at, :]).astype(BF)
    loc.finish(0)
    loc.start(1)
    for g in range(4):
        p_swap(g).wait_recv()
    join(pp, pr)
    for unit in p_units:
        unit.one.start()
    glob.finish(2)
    glob.start(3)
    for unit in u_units:
        unit.one.relay()
    for unit in d_units:
        unit.start2()
    gp[2, y] = gain_join(1)
    gain_swap(2)
    loc.finish(1)
    loc.start(2)
    for unit in p_units:
        unit.one.relay()
    for unit in u_units:
        unit.start2()
    for unit in d_units:
        unit.start3()
    loc.finish(2)
    loc.start(3)
    gp[3, z] = gain_join(2)
    gain_swap(3)
    for unit in p_units:
        unit.start2()
    for unit in u_units:
        unit.start3()
    for unit in p_units:
        unit.start3()
    glob.finish(3)
    glob.start(4)
    for i, unit in enumerate(d_units):
        down_o[:, pl.ds(*D_UNITS[i][:2])] = unit.three.finish()
    gain_o[...] = gain_join(3)
    loc.finish(3)
    loc.start(4)
    for i, unit in enumerate(u_units):
        up_o[:, pl.ds(*U_UNITS[i][:2])] = unit.three.finish()
    for i, unit in enumerate(p_units):
        first, width, _ = P_UNITS[i]
        value = unit.three.finish()
        proj_o[:, pl.ds(first, width)] = value[:8]
        proj_o[:, pl.ds(512 + first, width)] = value[8:]
    glob.finish(4)
    glob.drain()
    for unit in d_units + u_units + p_units:
        unit.drain()
    for half in range(2):
        await_send(ogp.at[seven, half], ab_sem.at[0], partner)
    for copy in x_og + [x_eg, x_r, x_el]:
        copy.wait_send()
    for i in range(4):
        t_swap(ht, 6, i).wait_send()
        t_swap(dat, 10, i).wait_send()
        p_swap(i).wait_send()
    loc.finish(4)
    loc.drain()


def finish(gog, table_g, table_l, gain, proj, up, down, gog_o, embg_o, embl_o, gain_o, proj_o, up_o, down_o, embg, embl, sem):
    pairs = ((gog, gog_o), (gain, gain_o), (proj, proj_o), (up, up_o), (down, down_o))
    copies = [pltpu.make_async_copy(src, dst, sem.at[n]) for n, (src, dst) in enumerate(pairs)]
    for copy in copies:
        copy.start()
    for n, (table, value, out) in enumerate(((table_g, embg, embg_o), (table_l, embl, embl_o))):
        for row in range(16):
            px, yh, c = row // 4, row // 2 % 2, row % 2
            for col in range(8):
                pz, yl = col // 2, col % 2
                value[row * 16 : row * 16 + 16, col * 128 : col * 128 + 128] = table[c, px, yh * 2 + yl, pz].astype(F32)
        copy = pltpu.make_async_copy(value, out, sem.at[5 + n])
        copy.start()
        copies.append(copy)
    for copy in copies:
        copy.wait()


def on_device(
    byte_ids,
    global_out,
    global_in_grad,
    out_grad,
    proj_weight,
    emb_local,
    norm_gain,
    up_weight,
    down_weight,
):
    scratch = [pltpu.VMEM(shape, kind) for _, shape, kind in FIXED]
    scratch += [pltpu.VMEM(shape, BF) for _, shape in TABLE] * 2
    for _, width, order in ALL_UNITS:
        scratch += unit_scratch(width, order)
    dma = pltpu.SemaphoreType.DMA
    scratch += [dma((n,)) for n in (N_LOADS, N_X, N_X, 3, 6, 10, 10)] + [dma((len(ALL_UNITS), 7))]
    vmem = pl.BlockSpec(memory_space=pltpu.VMEM)
    anywhere = pl.BlockSpec(memory_space=pl.ANY)
    parts = pl.pallas_call(
        kernel,
        out_shape=(
            pltpu.VMEM((256, 1024), BF),
            pltpu.VMEM((2, 4, 4, 4, 16, 128), BF),
            pltpu.VMEM((2, 4, 4, 4, 16, 128), BF),
            pltpu.VMEM((1, 1024), F32),
            pltpu.VMEM((8, 1024), F32),
            pltpu.VMEM((16, 1024), F32),
            pltpu.VMEM((16, 1024), F32),
        ),
        in_specs=[pl.BlockSpec(memory_space=pltpu.HBM)] * 9,
        out_specs=[vmem] * 7,
        scratch_shapes=scratch,
        compiler_params=pltpu.CompilerParams(
            collective_id=0, has_side_effects=True, vmem_limit_bytes=52 * 1024 * 1024
        ),
    )(
        pltpu.with_memory_space_constraint(byte_ids.T, pltpu.HBM),
        global_out,
        global_in_grad,
        out_grad,
        proj_weight,
        emb_local,
        pltpu.with_memory_space_constraint(norm_gain.reshape(1, 1024), pltpu.HBM),
        up_weight,
        down_weight,
    )
    out = jax.ShapeDtypeStruct
    gog, embg, embl, gain, proj, up, down = pl.pallas_call(
        finish,
        out_shape=(
            out((256, 1024), BF),
            out((256, 1024), F32),
            out((256, 1024), F32),
            out((1, 1024), F32),
            out((8, 1024), F32),
            out((16, 1024), F32),
            out((16, 1024), F32),
        ),
        in_specs=[vmem] * 7,
        out_specs=[anywhere] * 7,
        scratch_shapes=[pltpu.VMEM((256, 1024), F32), pltpu.VMEM((256, 1024), F32), dma((7,))],
        compiler_params=pltpu.CompilerParams(vmem_limit_bytes=6 * 1024 * 1024),
    )(*parts)
    return gog, embg, embl, gain.reshape(1024), proj.T, up.T, down


def solution(mesh):
    placed = (
        P("seq", None),
        P("seq", "tp"),
        P("seq", "tp"),
        P(("seq", "tp"), None),
        P(),
        P(),
        P(),
        P(),
        P(),
    )
    return jax.shard_map(
        on_device,
        mesh=mesh,
        in_specs=placed,
        out_specs=(
            P("seq", "tp"),
            P(),
            P(),
            P(),
            P(None, ("seq", "tp")),
            P(None, ("seq", "tp")),
            P(("seq", "tp"), None),
        ),
        check_vma=False,
    )
```

```python
import jax
import jax.numpy as jnp
from jax import lax
from jax.experimental import pallas as pl
from jax.experimental.pallas import tpu as pltpu
from jax.sharding import PartitionSpec as P

BF = jnp.bfloat16
F32 = jnp.float32
MESH = pl.DeviceIdType.MESH
ALL = slice(None)
D_UNITS = ((0, 256, (1, 2, 0)), (256, 384, (2, 0, 1)), (640, 384, (0, 1, 2)))
U_UNITS = ((0, 256, (0, 1, 2)), (256, 384, (1, 2, 0)), (640, 384, (2, 0, 1)))
P_UNITS = ((0, 128, (0, 1, 2)), (128, 256, (1, 2, 0)), (384, 128, (2, 1, 0)))
ALL_UNITS = D_UNITS + U_UNITS + P_UNITS
FAR_FIRST = (2, 1, 3)
PLANE = tuple((ky, kz) for ky in (2, 1, 3, 0) for kz in (2, 1, 3, 0) if ky or kz)


def mm(a, b):
    return lax.dot_general(a, b, (((1,), (0,)), ((), ())), preferred_element_type=F32)


def mm_nt(a, b):
    return lax.dot_general(a, b, (((1,), (1,)), ((), ())), preferred_element_type=F32)


def mm_tn(a, b):
    return lax.dot_general(a, b, (((0,), (0,)), ((), ())), preferred_element_type=F32)


def iota(shape, dim):
    return lax.broadcasted_iota(jnp.int32, shape, dim)


def remote(src, dst, send, recv, device):
    return pltpu.make_async_remote_copy(
        src_ref=src, dst_ref=dst, send_sem=send, recv_sem=recv, device_id=device, device_id_type=MESH
    )


def await_recv(ref, sem, device):
    remote(ref, ref, sem, sem, device).wait_recv()


def await_send(ref, sem, device):
    remote(ref, ref, sem, sem, device).wait_send()


class Ring:
    def __init__(self, src, cols, over, half, spot, device_at, buf, out, send, recv):
        self.src, self.cols, self.over, self.half = src, cols, over, half
        self.buf, self.out, self.send, self.recv = buf, out, send, recv
        here = spot[over]
        self.here, self.right, self.left, self.far = here, (here + 1) % 4, (here + 3) % 4, (here + 2) % 4
        self.to_right = device_at(over, self.right)
        self.to_left = device_at(over, self.left)

    def part(self, place, half):
        index = tuple(
            place if a == self.over else pl.ds(2 * half, 2) if a == self.half else ALL for a in (0, 1, 2)
        )
        return self.src.at[index + (ALL, pl.ds(*self.cols))]

    def start_far(self):
        remote(self.part(self.far, 0), self.buf.at[0], self.send, self.recv[0], self.to_right).start()
        remote(self.part(self.far, 1), self.buf.at[1], self.send, self.recv[0], self.to_left).start()

    def start_near(self):
        remote(self.part(self.right, 1), self.buf.at[2], self.send, self.recv[1], self.to_right).start()
        remote(self.part(self.left, 0), self.buf.at[3], self.send, self.recv[1], self.to_left).start()

    def start(self):
        self.start_far()
        self.start_near()

    def relay(self):
        await_recv(self.buf.at[pl.ds(0, 2)], self.recv[0], self.to_left)
        self.buf[0] = (self.buf[0].astype(F32) + self.part(self.right, 0)[...].astype(F32)).astype(BF)
        remote(self.buf.at[0], self.buf.at[4], self.send, self.recv[1], self.to_right).start()
        self.buf[1] = (self.buf[1].astype(F32) + self.part(self.left, 1)[...].astype(F32)).astype(BF)
        remote(self.buf.at[1], self.buf.at[5], self.send, self.recv[1], self.to_left).start()

    def out_half(self, half):
        index = tuple(pl.ds(2 * half, 2) if a == self.half else ALL for a in (0, 1, 2) if a != self.over)
        return self.out.at[index]

    def finish(self):
        await_recv(self.buf.at[pl.ds(2, 4)], self.recv[1], self.to_left)
        for half in range(2):
            self.out_half(half)[...] = (
                self.part(self.here, half)[...].astype(F32)
                + self.buf[4 + half].astype(F32)
                + self.buf[3 - half].astype(F32)
            ).astype(BF)

    def drain(self):
        await_send(self.buf, self.send, self.to_left)


class Direct:
    def __init__(self, src, axes, over, spot, device_at, buf, send, recv):
        self.src, self.axes, self.over, self.buf, self.send, self.recv = src, axes, over, buf, send, recv
        self.here = spot[over]
        self.device_at = device_at

    def part(self, place):
        return self.src.at[tuple(place if a == self.over else ALL for a in self.axes)]

    def start(self):
        for k in FAR_FIRST:
            there = (self.here + k) % 4
            self.to = self.device_at(self.over, there)
            remote(self.part(there), self.buf.at[k - 1], self.send, self.recv, self.to).start()

    def finish(self):
        await_recv(self.buf, self.recv, self.to)
        total = self.part(self.here)[...].astype(F32)
        for k in range(3):
            total = total + self.buf[k].astype(F32)
        return total

    def drain(self):
        await_send(self.buf, self.send, self.to)


class Unit:
    def __init__(self, src, cols, order, spot, device_at, bufs, sems):
        a, b, c = order
        first, out1, second, self.out2, last = bufs
        rest = tuple(n for n in (0, 1, 2) if n != a)
        self.one = Ring(src, cols, a, b, spot, device_at, first, out1, sems.at[0], (sems.at[1], sems.at[2]))
        self.two = Direct(out1, rest, b, spot, device_at, second, sems.at[3], sems.at[4])
        self.three = Direct(self.out2, (c,), c, spot, device_at, last, sems.at[5], sems.at[6])

    def start2(self):
        self.one.finish()
        self.two.start()

    def start3(self):
        self.out2[...] = self.two.finish().astype(BF)
        self.three.start()

    def drain(self):
        self.one.drain()
        self.two.drain()
        self.three.drain()


class Table:
    def __init__(self, bufs, gathered, spot, core, device, device_at, partner, sems):
        src, self.one, recv1, self.recv2 = bufs
        self.partner, self.sems = partner, sems
        x, y, z = spot
        self.spot = spot
        self.first = Direct(src, (0, 1, 2), 0, spot, device_at, recv1, sems.at[0], sems.at[1])
        self.own = (gathered.at[core, x, y, z], gathered.at[core, x], gathered.at[core])
        self.sized = (self.recv2, recv1, gathered.at[core])
        self.plane = []
        for ky, kz in PLANE:
            py, pz = (y + ky) % 4, (z + kz) % 4
            self.plane.append((py, pz, ky * 4 + kz - 1, device(x, py, pz, core)))
        self.to = (
            [there for _, _, _, there in self.plane],
            [device_at(0, (x + k) % 4) for k in FAR_FIRST],
            [partner],
        )

    def start(self, step):
        send, recv = self.sems.at[2 * step], self.sems.at[2 * step + 1]
        if step == 0:
            self.first.start()
        elif step == 1:
            for py, pz, n, there in self.plane:
                remote(self.one.at[py, pz], self.recv2.at[n], send, recv, there).start()
        else:
            n = step - 2
            for there in self.to[n]:
                remote(self.own[n], self.own[n], send, recv, there).start()

    def finish(self, step):
        if step == 0:
            self.one[...] = self.first.finish().astype(BF)
            return
        await_recv(self.recv2 if step == 1 else self.sized[step - 2], self.sems.at[2 * step + 1], self.partner)
        if step == 1:
            total = self.one[self.spot[1], self.spot[2]].astype(F32)
            for n in range(15):
                total = total + self.recv2[n].astype(F32)
            self.own[0][...] = total.astype(BF)

    def drain(self):
        self.first.drain()
        await_send(self.recv2, self.sems.at[2], self.partner)
        for n in range(3):
            await_send(self.sized[n], self.sems.at[2 * n + 4], self.partner)


def unit_scratch(width, order):
    a, b, c = order
    rest = tuple(n for n in (0, 1, 2) if n != a)
    one = tuple(2 if n == b else 4 for n in rest)
    return [
        pltpu.VMEM((6,) + one + (16, width), BF),
        pltpu.VMEM((4, 4, 16, width), BF),
        pltpu.VMEM((3, 4, 16, width), BF),
        pltpu.VMEM((4, 16, width), BF),
        pltpu.VMEM((3, 16, width), BF),
    ]


FIXED = (
    ("ids", (8, 256), jnp.int32),
    ("gain", (1, 1024), F32),
    ("og", (256, 1024), BF),
    ("dn", (2048, 1024), BF),
    ("gig", (256, 1024), BF),
    ("pw", (1024, 1024), BF),
    ("emb", (256, 1024), BF),
    ("up", (1024, 2048), BF),
    ("ogp", (8, 2, 16, 1024), BF),
    ("og2", (2, 8, 2, 16, 1024), BF),
    ("slot", (256, 1024), BF),
    ("slope", (8, 256, 256), F32),
    ("norm", (256, 1024), F32),
    ("scale", (256, 128), F32),
    ("r2", (512, 1024), BF),
    ("hot", (256, 256), BF),
    ("ht", (2, 1024, 512), BF),
    ("dat", (2, 1024, 512), BF),
    ("da", (256, 2048), BF),
    ("dr", (256, 1024), F32),
    ("du", (256, 1024), BF),
    ("dut", (1024, 256), BF),
    ("dp", (4, 4, 4, 16, 1024), BF),
    ("upart", (4, 4, 4, 16, 1024), BF),
    ("pp", (2, 4, 4, 4, 16, 512), BF),
    ("pr", (4, 4, 4, 16, 512), BF),
    ("gp", (4, 4, 1, 1024), F32),
)
TABLE = (
    ("part", (2, 4, 4, 4, 16, 128)),
    ("src", (4, 4, 4, 16, 128)),
    ("one", (4, 4, 16, 128)),
    ("recv1", (3, 4, 4, 16, 128)),
    ("recv2", (15, 16, 128)),
)
N_LOADS, N_X = 10, 18


def kernel(*refs):
    ids_h, go_h, gig_h, og_h, pw_h, emb_h, gain_h, up_h, dn_h = refs[:9]
    gog_o, table_g, table_l, gain_o, proj_o, up_o, down_o = refs[9:16]
    rest = list(refs[16:])
    buf = {name: rest.pop(0) for name, _, _ in FIXED}
    eg = {name: rest.pop(0) for name, _ in TABLE}
    el = {name: rest.pop(0) for name, _ in TABLE}
    unit_bufs = []
    for _ in ALL_UNITS:
        unit_bufs.append([rest.pop(0) for _ in range(5)])
    load_sem, x_send, x_recv, ab_sem, g_sem, tg_sem, tl_sem, u_sem = rest
    ids, gain = buf["ids"], buf["gain"]
    og, dn, gig, pw, emb, up = (buf[n] for n in ("og", "dn", "gig", "pw", "emb", "up"))
    og2, slot, slope, norm, scale, r2 = (buf[n] for n in ("og2", "slot", "slope", "norm", "scale", "r2"))
    hot, ht, dat, da = (buf[n] for n in ("hot", "ht", "dat", "da"))
    dr, du, dut, dp, upart, pp = (buf[n] for n in ("dr", "du", "dut", "dp", "upart", "pp"))
    pr, gp, ogp = (buf[n] for n in ("pr", "gp", "ogp"))

    seq = lax.axis_index("seq")
    tp = lax.axis_index("tp")
    core = seq % 2
    other = 1 - core
    x = seq // 4
    y = (seq // 2) % 2 * 2 + tp % 2
    z = tp // 2
    spot = (x, y, z)

    def device(px, py, pz, pc):
        return ((px * 2 + py // 2) * 2 + pc, pz * 2 + py % 2)

    def device_at(axis, place):
        where = list(spot)
        where[axis] = place
        return device(*where, core)

    partner = device(x, y, z, other)

    barrier = pltpu.get_barrier_semaphore()
    pl.semaphore_signal(barrier, inc=1, device_id=partner, device_id_type=MESH)
    for ky, kz in PLANE:
        there = device(x, (y + ky) % 4, (z + kz) % 4, core)
        pl.semaphore_signal(barrier, inc=1, device_id=there, device_id_type=MESH)
    for k in FAR_FIRST:
        pl.semaphore_signal(barrier, inc=1, device_id=device_at(0, (x + k) % 4), device_id_type=MESH)
    loads = {}
    for n, group in enumerate(
        (
            (("og", og_h, og),),
            (("slot", go_h, slot),),
            (("pw", pw_h, pw),),
            (("ids", ids_h, ids),),
            (("emb", emb_h, emb),),
            (("gain", gain_h, gain),),
            (("gig", gig_h, gig),),
            (("up", up_h, up),),
            (("dn", dn_h, dn),),
        )
    ):
        for name, src, dst in group:
            loads[name] = pltpu.make_async_copy(src, dst, load_sem.at[n])
            loads[name].start()

    loads["og"].wait()
    row, col = iota((256, 256), 0), iota((256, 256), 1)
    own, far = pl.ds(0, 256), pl.ds(256, 256)
    perm = (col == 8 * (row % 32) + row // 32).astype(BF)
    ogp[...] = mm(perm, og[...]).astype(BF).reshape(8, 2, 16, 1024)
    keep = pltpu.make_async_copy(ogp.at[tp], og2.at[0, tp], load_sem.at[9])
    keep.start()
    pl.semaphore_wait(barrier, 19)
    for half in range(2):
        for k in range(1, 8):
            there = (tp + k) % 8
            remote(
                ogp.at[there, half], og2.at[0, tp, half], ab_sem.at[0], ab_sem.at[1 + half], (seq, there)
            ).start()

    def swap(n, src, dst):
        copy = remote(src, dst, x_send.at[n], x_recv.at[n], partner)
        copy.start()
        return copy

    loads["ids"].wait()
    ids_v = ids[...]
    row8 = iota((8, 256), 0)
    own_id = jnp.sum(jnp.where(row8 == tp, ids_v, 0), axis=0, keepdims=True)
    hot_own = (row == own_id).astype(BF)
    prev_id = jnp.sum(jnp.where(row8 == tp - 1, ids_v, 0), axis=0, keepdims=True) - (tp == 0).astype(jnp.int32)
    hot[...] = (row == prev_id).astype(BF)

    def table_of(bufs, gathered, sems):
        order = tuple(bufs[n] for n in ("src", "one", "recv1", "recv2"))
        return Table(order, gathered, spot, core, device, device_at, partner, sems)

    glob, loc = table_of(eg, table_g, tg_sem), table_of(el, table_l, tl_sem)

    def put_table(part, n, value):
        block = value.astype(BF).reshape(4, 2, 2, 16, 256)
        for c in range(2):
            for yh in range(2):
                for yl in range(2):
                    part[c, :, yh * 2 + yl, n] = block[:, yh, c, :, yl * 128 : yl * 128 + 128]

    def join(part, src):
        def step(i, carry):
            src[i] = (src[i].astype(F32) + part[core, i].astype(F32)).astype(BF)
            return carry

        lax.fori_loop(0, 4, step, 0)

    loads["gig"].wait()
    for n in range(4):
        put_table(eg["part"], n, mm(hot_own, gig[:, n * 256 : n * 256 + 256]))
    x_eg = swap(1, eg["part"].at[other], eg["src"])

    loads["pw"].wait()
    loads["emb"].wait()
    loads["slot"].wait()
    loads["gain"].wait()
    square = jnp.zeros((256, 1), F32)
    for n in range(4):
        at = slice(n * 256, n * 256 + 256)
        u_part = mm(slot[...], pw[:, at]) + mm_tn(hot[...], emb[:, at])
        norm[:, at] = u_part
        square = square + jnp.sum(u_part * u_part, axis=1, keepdims=True)
    scale_v = lax.rsqrt(square * (1.0 / 1024.0) + 1e-05)
    scale[...] = jnp.broadcast_to(scale_v, (256, 128))
    for n in range(4):
        at = slice(n * 256, n * 256 + 256)
        normed = norm[:, at] * scale_v
        norm[:, at] = normed
        r2[own, at] = (normed * gain[:, at]).astype(BF)
    x_r = swap(2, r2.at[own], r2.at[far])
    x_eg.wait_recv()
    join(eg["part"], eg["src"])
    glob.start(0)

    def t_swap(ref, base, j):
        rows = pl.ds(pl.multiple_of(j * 256, 256), 256)
        return remote(
            ref.at[other, rows, own], ref.at[other, rows, far], x_send.at[base + j], x_recv.at[base + j], partner
        )

    loads["up"].wait()

    def ff_step(j, carry):
        for k2 in range(2):
            k = j * 2 + k2
            at = pl.ds(pl.multiple_of(k * 256, 256), 256)
            rows = pl.ds(pl.multiple_of(k * 128, 128), 128)
            a = mm(r2[own, :], up[:, at])
            sig = jax.nn.sigmoid(a)
            h_t = (a * sig).astype(BF).T
            ht[0, rows, own] = h_t[:128]
            ht[1, rows, own] = h_t[128:]
            slope[k] = sig * (1.0 + a * (1.0 - sig))
        t_swap(ht, 6, j).start()
        return carry

    lax.fori_loop(0, 4, ff_step, 0)

    def da_step(j, carry):
        for k2 in range(2):
            k = j * 2 + k2
            at = pl.ds(pl.multiple_of(k * 256, 256), 256)
            rows = pl.ds(pl.multiple_of(k * 128, 128), 128)
            da_v = (mm_nt(og2[0].reshape(256, 1024), dn[at, :]) * slope[k]).astype(BF)
            da[:, at] = da_v
            da_t = da_v.T
            dat[0, rows, own] = da_t[:128]
            dat[1, rows, own] = da_t[128:]
        t_swap(dat, 10, j).start()
        return carry

    loads["dn"].wait()
    keep.wait()
    seven = pl.ds(0, 7)
    x_og = []
    for half in range(2):
        await_recv(og2.at[0, seven, half], ab_sem.at[1 + half], partner)
        x_og.append(swap((0, 4)[half], og2.at[0, :, half], og2.at[1, :, half]))
    lax.fori_loop(0, 2, da_step, 0)

    def units(src, table, first):
        return [
            Unit(src, t[:2], t[2], spot, device_at, unit_bufs[first + i], u_sem.at[first + i])
            for i, t in enumerate(table)
        ]

    d_units = units(dp, D_UNITS, 0)
    u_units = units(upart, U_UNITS, 3)
    p_units = units(pr, P_UNITS, 6)

    def big(lhs, rhs, out, n):
        at = slice(n * 256, n * 256 + 256)

        def step(g):
            rows = pl.ds(g * 512, 512)
            v = mm(lhs[core, rows, :], rhs(at)).astype(BF).reshape(2, 2, 4, 2, 16, 256)
            for xx in range(2):
                for yh in range(2):
                    for yl in range(2):
                        out[2 * g + xx, yh * 2 + yl, :, :, at] = v[xx, yh, :, yl]

        step(0)
        step(1)

    for j in range(4):
        t_swap(ht, 6, j).wait_recv()
    for copy in x_og:
        copy.wait_recv()

    def both_og(at):
        return og2[:, :, :, :, at].reshape(512, 256)

    def both_r(at):
        return r2[:, at]

    big(ht, both_og, dp, 0)
    d_units[0].one.start()
    big(ht, both_og, dp, 1)
    big(ht, both_og, dp, 2)
    d_units[1].one.start()
    big(ht, both_og, dp, 3)
    d_units[2].one.start()
    glob.finish(0)
    glob.start(1)
    lax.fori_loop(2, 4, da_step, 0)
    for n in range(4):
        at = slice(n * 256, n * 256 + 256)
        dr[:, at] = mm_nt(da[...], up[at, :])
    gain_v = gain[...]

    def du_step(i, total):
        rows = pl.ds(pl.multiple_of(i * 32, 32), 32)
        dr_v = dr[rows, :]
        normed = norm[rows, :]
        product = dr_v * normed
        dn_v = dr_v * gain_v
        mean = jnp.sum(product * gain_v, axis=1, keepdims=True) * (1.0 / 1024.0)
        du_v = og2[0, i].reshape(32, 1024).astype(F32) + scale[rows, 0:1] * (dn_v - normed * mean)
        du[rows, :] = du_v.astype(BF)
        return total + jnp.sum(product.reshape(4, 8, 1024), axis=0)

    gain_part = lax.fori_loop(0, 8, du_step, jnp.zeros((8, 1024), F32))
    for n in range(4):
        put_table(el["part"], n, mm(hot[...], du[:, n * 256 : n * 256 + 256]))
    x_el = swap(3, el["part"].at[other], el["src"])
    gp[0, core] = jnp.sum(gain_part, axis=0, keepdims=True)
    x_g = swap(5, gp.at[0, core], gp.at[0, core])
    for unit in d_units:
        unit.one.relay()
    x_el.wait_recv()
    join(el["part"], el["src"])
    loc.start(0)
    x_r.wait_recv()
    for j in range(4):
        t_swap(dat, 10, j).wait_recv()
    big(dat, both_r, upart, 0)
    u_units[0].one.start()
    big(dat, both_r, upart, 1)
    big(dat, both_r, upart, 2)
    u_units[1].one.start()
    big(dat, both_r, upart, 3)
    u_units[2].one.start()
    glob.finish(1)
    glob.start(2)
    for n in range(4):
        at = slice(n * 256, n * 256 + 256)
        dut[at, :] = du[:, at].T

    def gain_swap(step):
        axis = step - 1
        mine = gp.at[step, spot[axis]]
        for k in FAR_FIRST:
            device = device_at(axis, (spot[axis] + k) % 4)
            remote(mine, mine, g_sem.at[2 * axis], g_sem.at[2 * axis + 1], device).start()

    def gain_join(step):
        three = gp.at[step, pl.ds(0, 3)]
        await_recv(three, g_sem.at[2 * step - 1], partner)
        await_send(three, g_sem.at[2 * step - 2], partner)
        return gp[step, 0] + gp[step, 1] + gp[step, 2] + gp[step, 3]

    def p_swap(g):
        return remote(pp.at[other, g], pr.at[g], x_send.at[14 + g], x_recv.at[14 + g], partner)

    def proj_step(g, carry):
        rows = pl.ds(pl.multiple_of(g * 256, 256), 256)
        for n in range(2):
            lo, hi = slice(n * 256, n * 256 + 256), slice(512 + n * 256, 768 + n * 256)
            v_lo = mm(dut[rows, :], slot[:, lo]).reshape(2, 2, 4, 2, 8, 256)
            v_hi = mm(dut[rows, :], slot[:, hi]).reshape(2, 2, 4, 2, 8, 256)
            v = jnp.concatenate([v_lo, v_hi], axis=4).astype(BF)
            for c in range(2):
                for yh in range(2):
                    for yl in range(2):
                        pp[c, g, yh * 2 + yl, :, :, lo] = v[yh, c, :, yl]
        p_swap(g).start()
        return carry

    lax.fori_loop(0, 4, proj_step, 0)
    x_g.wait_recv()
    x_g.wait_send()
    gp[1, x] = gp[0, 0] + gp[0, 1]
    gain_swap(1)
    for n in range(4):
        at = slice(n * 256, n * 256 + 256)
        gog_o[:, at] = mm_nt(du[...], pw[at, :]).astype(BF)
    loc.finish(0)
    loc.start(1)
    for g in range(4):
        p_swap(g).wait_recv()
    join(pp, pr)
    for unit in p_units:
        unit.one.start_far()
    for unit in u_units:
        unit.one.relay()
    for unit in p_units:
        unit.one.start_near()
    for unit in d_units:
        unit.start2()
    for unit in p_units:
        unit.one.relay()
    loc.finish(1)
    loc.start(2)
    glob.finish(2)
    glob.start(3)
    for unit in u_units:
        unit.start2()
    gp[2, y] = gain_join(1)
    gain_swap(2)
    for unit in p_units:
        unit.start2()
    loc.finish(2)
    loc.start(3)
    for unit in d_units:
        unit.start3()
    for unit in u_units:
        unit.start3()
    gp[3, z] = gain_join(2)
    gain_swap(3)
    for unit in p_units:
        unit.start3()
    glob.finish(3)
    glob.start(4)
    for i, unit in enumerate(d_units):
        down_o[:, pl.ds(*D_UNITS[i][:2])] = unit.three.finish()
    gain_o[...] = gain_join(3)
    loc.finish(3)
    loc.start(4)
    for i, unit in enumerate(u_units):
        up_o[:, pl.ds(*U_UNITS[i][:2])] = unit.three.finish()
    for i, unit in enumerate(p_units):
        first, width, _ = P_UNITS[i]
        value = unit.three.finish()
        proj_o[:, pl.ds(first, width)] = value[:8]
        proj_o[:, pl.ds(512 + first, width)] = value[8:]
    glob.finish(4)
    glob.drain()
    for unit in d_units + u_units + p_units:
        unit.drain()
    for half in range(2):
        await_send(ogp.at[seven, half], ab_sem.at[0], partner)
    for copy in x_og + [x_eg, x_r, x_el]:
        copy.wait_send()
    for i in range(4):
        t_swap(ht, 6, i).wait_send()
        t_swap(dat, 10, i).wait_send()
        p_swap(i).wait_send()
    loc.finish(4)
    loc.drain()


def finish(gog, table_g, table_l, gain, proj, up, down, gog_o, embg_o, embl_o, gain_o, proj_o, up_o, down_o, embg, embl, sem):
    pairs = ((gog, gog_o), (gain, gain_o), (proj, proj_o), (up, up_o), (down, down_o))
    copies = [pltpu.make_async_copy(src, dst, sem.at[n]) for n, (src, dst) in enumerate(pairs)]
    for copy in copies:
        copy.start()
    for n, (table, value, out) in enumerate(((table_g, embg, embg_o), (table_l, embl, embl_o))):
        for row in range(16):
            px, yh, c = row // 4, row // 2 % 2, row % 2
            for col in range(8):
                pz, yl = col // 2, col % 2
                value[row * 16 : row * 16 + 16, col * 128 : col * 128 + 128] = table[c, px, yh * 2 + yl, pz].astype(F32)
        copy = pltpu.make_async_copy(value, out, sem.at[5 + n])
        copy.start()
        copies.append(copy)
    for copy in copies:
        copy.wait()


def on_device(
    byte_ids,
    global_out,
    global_in_grad,
    out_grad,
    proj_weight,
    emb_local,
    norm_gain,
    up_weight,
    down_weight,
):
    scratch = [pltpu.VMEM(shape, kind) for _, shape, kind in FIXED]
    scratch += [pltpu.VMEM(shape, BF) for _, shape in TABLE] * 2
    for _, width, order in ALL_UNITS:
        scratch += unit_scratch(width, order)
    dma = pltpu.SemaphoreType.DMA
    scratch += [dma((n,)) for n in (N_LOADS, N_X, N_X, 3, 6, 10, 10)] + [dma((len(ALL_UNITS), 7))]
    vmem = pl.BlockSpec(memory_space=pltpu.VMEM)
    anywhere = pl.BlockSpec(memory_space=pl.ANY)
    parts = pl.pallas_call(
        kernel,
        out_shape=(
            pltpu.VMEM((256, 1024), BF),
            pltpu.VMEM((2, 4, 4, 4, 16, 128), BF),
            pltpu.VMEM((2, 4, 4, 4, 16, 128), BF),
            pltpu.VMEM((1, 1024), F32),
            pltpu.VMEM((8, 1024), F32),
            pltpu.VMEM((16, 1024), F32),
            pltpu.VMEM((16, 1024), F32),
        ),
        in_specs=[pl.BlockSpec(memory_space=pltpu.HBM)] * 9,
        out_specs=[vmem] * 7,
        scratch_shapes=scratch,
        compiler_params=pltpu.CompilerParams(
            collective_id=0, has_side_effects=True, vmem_limit_bytes=52 * 1024 * 1024
        ),
    )(
        pltpu.with_memory_space_constraint(byte_ids.T, pltpu.HBM),
        global_out,
        global_in_grad,
        out_grad,
        proj_weight,
        emb_local,
        pltpu.with_memory_space_constraint(norm_gain.reshape(1, 1024), pltpu.HBM),
        up_weight,
        down_weight,
    )
    out = jax.ShapeDtypeStruct
    gog, embg, embl, gain, proj, up, down = pl.pallas_call(
        finish,
        out_shape=(
            out((256, 1024), BF),
            out((256, 1024), F32),
            out((256, 1024), F32),
            out((1, 1024), F32),
            out((8, 1024), F32),
            out((16, 1024), F32),
            out((16, 1024), F32),
        ),
        in_specs=[vmem] * 7,
        out_specs=[anywhere] * 7,
        scratch_shapes=[pltpu.VMEM((256, 1024), F32), pltpu.VMEM((256, 1024), F32), dma((7,))],
        compiler_params=pltpu.CompilerParams(vmem_limit_bytes=6 * 1024 * 1024),
    )(*parts)
    return gog, embg, embl, gain.reshape(1024), proj.T, up.T, down


def solution(mesh):
    placed = (
        P("seq", None),
        P("seq", "tp"),
        P("seq", "tp"),
        P(("seq", "tp"), None),
        P(),
        P(),
        P(),
        P(),
        P(),
    )
    return jax.shard_map(
        on_device,
        mesh=mesh,
        in_specs=placed,
        out_specs=(
            P("seq", "tp"),
            P(),
            P(),
            P(),
            P(None, ("seq", "tp")),
            P(None, ("seq", "tp")),
            P(("seq", "tp"), None),
        ),
        check_vma=False,
    )
```

```python
import jax
import jax.numpy as jnp
from jax import lax
from jax.experimental import pallas as pl
from jax.experimental.pallas import tpu as pltpu
from jax.sharding import PartitionSpec as P

BF = jnp.bfloat16
F32 = jnp.float32
MESH = pl.DeviceIdType.MESH
ALL = slice(None)
D_UNITS = ((0, 256, (1, 2, 0)), (256, 384, (2, 0, 1)), (640, 384, (0, 1, 2)))
U_UNITS = ((0, 256, (0, 1, 2)), (256, 384, (1, 2, 0)), (640, 384, (2, 0, 1)))
P_UNITS = ((0, 128, (0, 1, 2)), (128, 256, (1, 2, 0)), (384, 128, (2, 1, 0)))
ALL_UNITS = D_UNITS + U_UNITS + P_UNITS
FAR_FIRST = (2, 1, 3)
PLANE = tuple((ky, kz) for ky in (2, 1, 3, 0) for kz in (2, 1, 3, 0) if ky or kz)


def mm(a, b):
    return lax.dot_general(a, b, (((1,), (0,)), ((), ())), preferred_element_type=F32)


def mm_nt(a, b):
    return lax.dot_general(a, b, (((1,), (1,)), ((), ())), preferred_element_type=F32)


def mm_tn(a, b):
    return lax.dot_general(a, b, (((0,), (0,)), ((), ())), preferred_element_type=F32)


def iota(shape, dim):
    return lax.broadcasted_iota(jnp.int32, shape, dim)


def remote(src, dst, send, recv, device):
    return pltpu.make_async_remote_copy(
        src_ref=src, dst_ref=dst, send_sem=send, recv_sem=recv, device_id=device, device_id_type=MESH
    )


def await_recv(ref, sem, device):
    remote(ref, ref, sem, sem, device).wait_recv()


def await_send(ref, sem, device):
    remote(ref, ref, sem, sem, device).wait_send()


class Ring:
    def __init__(self, src, cols, over, half, spot, device_at, buf, out, send, recv):
        self.src, self.cols, self.over, self.half = src, cols, over, half
        self.buf, self.out, self.send, self.recv = buf, out, send, recv
        here = spot[over]
        self.here, self.right, self.left, self.far = here, (here + 1) % 4, (here + 3) % 4, (here + 2) % 4
        self.to_right = device_at(over, self.right)
        self.to_left = device_at(over, self.left)

    def part(self, place, half):
        index = tuple(
            place if a == self.over else pl.ds(2 * half, 2) if a == self.half else ALL for a in (0, 1, 2)
        )
        return self.src.at[index + (ALL, pl.ds(*self.cols))]

    def start_far(self):
        remote(self.part(self.far, 0), self.buf.at[0], self.send, self.recv[0], self.to_right).start()
        remote(self.part(self.far, 1), self.buf.at[1], self.send, self.recv[0], self.to_left).start()

    def start_near(self):
        remote(self.part(self.right, 1), self.buf.at[2], self.send, self.recv[1], self.to_right).start()
        remote(self.part(self.left, 0), self.buf.at[3], self.send, self.recv[1], self.to_left).start()

    def start(self):
        self.start_far()
        self.start_near()

    def relay(self):
        await_recv(self.buf.at[pl.ds(0, 2)], self.recv[0], self.to_left)
        self.buf[0] = (self.buf[0].astype(F32) + self.part(self.right, 0)[...].astype(F32)).astype(BF)
        remote(self.buf.at[0], self.buf.at[4], self.send, self.recv[1], self.to_right).start()
        self.buf[1] = (self.buf[1].astype(F32) + self.part(self.left, 1)[...].astype(F32)).astype(BF)
        remote(self.buf.at[1], self.buf.at[5], self.send, self.recv[1], self.to_left).start()

    def out_half(self, half):
        index = tuple(pl.ds(2 * half, 2) if a == self.half else ALL for a in (0, 1, 2) if a != self.over)
        return self.out.at[index]

    def finish(self):
        await_recv(self.buf.at[pl.ds(2, 4)], self.recv[1], self.to_left)
        for half in range(2):
            self.out_half(half)[...] = (
                self.part(self.here, half)[...].astype(F32)
                + self.buf[4 + half].astype(F32)
                + self.buf[3 - half].astype(F32)
            ).astype(BF)

    def drain(self):
        await_send(self.buf, self.send, self.to_left)


class Direct:
    def __init__(self, src, axes, over, spot, device_at, buf, send, recv):
        self.src, self.axes, self.over, self.buf, self.send, self.recv = src, axes, over, buf, send, recv
        self.here = spot[over]
        self.device_at = device_at

    def part(self, place):
        return self.src.at[tuple(place if a == self.over else ALL for a in self.axes)]

    def start(self):
        for k in FAR_FIRST:
            there = (self.here + k) % 4
            self.to = self.device_at(self.over, there)
            remote(self.part(there), self.buf.at[k - 1], self.send, self.recv, self.to).start()

    def finish(self):
        await_recv(self.buf, self.recv, self.to)
        total = self.part(self.here)[...].astype(F32)
        for k in range(3):
            total = total + self.buf[k].astype(F32)
        return total

    def drain(self):
        await_send(self.buf, self.send, self.to)


class Unit:
    def __init__(self, src, cols, order, spot, device_at, bufs, sems):
        a, b, c = order
        first, out1, second, self.out2, last = bufs
        rest = tuple(n for n in (0, 1, 2) if n != a)
        self.one = Ring(src, cols, a, b, spot, device_at, first, out1, sems.at[0], (sems.at[1], sems.at[2]))
        self.two = Direct(out1, rest, b, spot, device_at, second, sems.at[3], sems.at[4])
        self.three = Direct(self.out2, (c,), c, spot, device_at, last, sems.at[5], sems.at[6])

    def start2(self):
        self.one.finish()
        self.two.start()

    def start3(self):
        self.out2[...] = self.two.finish().astype(BF)
        self.three.start()

    def drain(self):
        self.one.drain()
        self.two.drain()
        self.three.drain()


class Table:
    def __init__(self, bufs, gathered, spot, core, device, device_at, partner, sems):
        src, self.one, recv1, self.recv2 = bufs
        self.partner, self.sems = partner, sems
        x, y, z = spot
        self.spot = spot
        self.first = Direct(src, (0, 1, 2), 0, spot, device_at, recv1, sems.at[0], sems.at[1])
        self.own = (gathered.at[core, x, y, z], gathered.at[core, x], gathered.at[core])
        self.sized = (self.recv2, recv1, gathered.at[core])
        self.plane = []
        for ky, kz in PLANE:
            py, pz = (y + ky) % 4, (z + kz) % 4
            self.plane.append((py, pz, ky * 4 + kz - 1, device(x, py, pz, core)))
        self.to = (
            [there for _, _, _, there in self.plane],
            [device_at(0, (x + k) % 4) for k in FAR_FIRST],
            [partner],
        )

    def start(self, step):
        send, recv = self.sems.at[2 * step], self.sems.at[2 * step + 1]
        if step == 0:
            self.first.start()
        elif step == 1:
            for py, pz, n, there in self.plane:
                remote(self.one.at[py, pz], self.recv2.at[n], send, recv, there).start()
        else:
            n = step - 2
            for there in self.to[n]:
                remote(self.own[n], self.own[n], send, recv, there).start()

    def finish(self, step):
        if step == 0:
            self.one[...] = self.first.finish().astype(BF)
            return
        await_recv(self.recv2 if step == 1 else self.sized[step - 2], self.sems.at[2 * step + 1], self.partner)
        if step == 1:
            total = self.one[self.spot[1], self.spot[2]].astype(F32)
            for n in range(15):
                total = total + self.recv2[n].astype(F32)
            self.own[0][...] = total.astype(BF)

    def drain(self):
        self.first.drain()
        await_send(self.recv2, self.sems.at[2], self.partner)
        for n in range(3):
            await_send(self.sized[n], self.sems.at[2 * n + 4], self.partner)


def unit_scratch(width, order):
    a, b, c = order
    rest = tuple(n for n in (0, 1, 2) if n != a)
    one = tuple(2 if n == b else 4 for n in rest)
    return [
        pltpu.VMEM((6,) + one + (16, width), BF),
        pltpu.VMEM((4, 4, 16, width), BF),
        pltpu.VMEM((3, 4, 16, width), BF),
        pltpu.VMEM((4, 16, width), BF),
        pltpu.VMEM((3, 16, width), BF),
    ]


FIXED = (
    ("ids", (8, 256), jnp.int32),
    ("gain", (1, 1024), F32),
    ("og", (256, 1024), BF),
    ("dn", (2048, 1024), BF),
    ("gig", (256, 1024), BF),
    ("pw", (1024, 1024), BF),
    ("emb", (256, 1024), BF),
    ("up", (1024, 2048), BF),
    ("ogp", (8, 2, 16, 1024), BF),
    ("og2", (2, 8, 2, 16, 1024), BF),
    ("slot", (256, 1024), BF),
    ("slope", (8, 256, 256), F32),
    ("norm", (256, 1024), F32),
    ("scale", (256, 128), F32),
    ("r2", (512, 1024), BF),
    ("hot", (256, 256), BF),
    ("ht", (2, 1024, 512), BF),
    ("dat", (2, 1024, 512), BF),
    ("da", (256, 2048), BF),
    ("dr", (256, 1024), F32),
    ("du", (256, 1024), BF),
    ("dut", (1024, 256), BF),
    ("dp", (4, 4, 4, 16, 1024), BF),
    ("upart", (4, 4, 4, 16, 1024), BF),
    ("pp", (2, 4, 4, 4, 16, 512), BF),
    ("pr", (4, 4, 4, 16, 512), BF),
    ("gp", (4, 4, 1, 1024), F32),
)
TABLE = (
    ("part", (2, 4, 4, 4, 16, 128)),
    ("src", (4, 4, 4, 16, 128)),
    ("one", (4, 4, 16, 128)),
    ("recv1", (3, 4, 4, 16, 128)),
    ("recv2", (15, 16, 128)),
)
N_LOADS, N_X = 10, 18


def kernel(*refs):
    ids_h, go_h, gig_h, og_h, pw_h, emb_h, gain_h, up_h, dn_h = refs[:9]
    gog_o, table_g, table_l, gain_o, proj_o, up_o, down_o = refs[9:16]
    rest = list(refs[16:])
    buf = {name: rest.pop(0) for name, _, _ in FIXED}
    eg = {name: rest.pop(0) for name, _ in TABLE}
    el = {name: rest.pop(0) for name, _ in TABLE}
    unit_bufs = []
    for _ in ALL_UNITS:
        unit_bufs.append([rest.pop(0) for _ in range(5)])
    load_sem, x_send, x_recv, ab_sem, g_sem, tg_sem, tl_sem, u_sem = rest
    ids, gain = buf["ids"], buf["gain"]
    og, dn, gig, pw, emb, up = (buf[n] for n in ("og", "dn", "gig", "pw", "emb", "up"))
    og2, slot, slope, norm, scale, r2 = (buf[n] for n in ("og2", "slot", "slope", "norm", "scale", "r2"))
    hot, ht, dat, da = (buf[n] for n in ("hot", "ht", "dat", "da"))
    dr, du, dut, dp, upart, pp = (buf[n] for n in ("dr", "du", "dut", "dp", "upart", "pp"))
    pr, gp, ogp = (buf[n] for n in ("pr", "gp", "ogp"))

    seq = lax.axis_index("seq")
    tp = lax.axis_index("tp")
    core = seq % 2
    other = 1 - core
    x = seq // 4
    y = (seq // 2) % 2 * 2 + tp % 2
    z = tp // 2
    spot = (x, y, z)

    def device(px, py, pz, pc):
        return ((px * 2 + py // 2) * 2 + pc, pz * 2 + py % 2)

    def device_at(axis, place):
        where = list(spot)
        where[axis] = place
        return device(*where, core)

    partner = device(x, y, z, other)

    barrier = pltpu.get_barrier_semaphore()
    pl.semaphore_signal(barrier, inc=1, device_id=partner, device_id_type=MESH)
    for ky, kz in PLANE:
        there = device(x, (y + ky) % 4, (z + kz) % 4, core)
        pl.semaphore_signal(barrier, inc=1, device_id=there, device_id_type=MESH)
    for k in FAR_FIRST:
        pl.semaphore_signal(barrier, inc=1, device_id=device_at(0, (x + k) % 4), device_id_type=MESH)
    loads = {}
    for n, group in enumerate(
        (
            (("og", og_h, og),),
            (("slot", go_h, slot),),
            (("pw", pw_h, pw),),
            (("ids", ids_h, ids),),
            (("emb", emb_h, emb),),
            (("gain", gain_h, gain),),
            (("gig", gig_h, gig),),
            (("up", up_h, up),),
            (("dn", dn_h, dn),),
        )
    ):
        for name, src, dst in group:
            loads[name] = pltpu.make_async_copy(src, dst, load_sem.at[n])
            loads[name].start()

    loads["og"].wait()
    row, col = iota((256, 256), 0), iota((256, 256), 1)
    own, far = pl.ds(0, 256), pl.ds(256, 256)
    perm = (col == 8 * (row % 32) + row // 32).astype(BF)
    ogp[...] = mm(perm, og[...]).astype(BF).reshape(8, 2, 16, 1024)
    keep = pltpu.make_async_copy(ogp.at[tp], og2.at[0, tp], load_sem.at[9])
    keep.start()
    pl.semaphore_wait(barrier, 19)
    for half in range(2):
        for k in range(1, 8):
            there = (tp + k) % 8
            remote(
                ogp.at[there, half], og2.at[0, tp, half], ab_sem.at[0], ab_sem.at[1 + half], (seq, there)
            ).start()

    def swap(n, src, dst):
        copy = remote(src, dst, x_send.at[n], x_recv.at[n], partner)
        copy.start()
        return copy

    loads["ids"].wait()
    ids_v = ids[...]
    row8 = iota((8, 256), 0)
    own_id = jnp.sum(jnp.where(row8 == tp, ids_v, 0), axis=0, keepdims=True)
    hot_own = (row == own_id).astype(BF)
    prev_id = jnp.sum(jnp.where(row8 == tp - 1, ids_v, 0), axis=0, keepdims=True) - (tp == 0).astype(jnp.int32)
    hot[...] = (row == prev_id).astype(BF)

    def table_of(bufs, gathered, sems):
        order = tuple(bufs[n] for n in ("src", "one", "recv1", "recv2"))
        return Table(order, gathered, spot, core, device, device_at, partner, sems)

    glob, loc = table_of(eg, table_g, tg_sem), table_of(el, table_l, tl_sem)

    def put_table(part, n, value):
        block = value.astype(BF).reshape(4, 2, 2, 16, 256)
        for c in range(2):
            for yh in range(2):
                for yl in range(2):
                    part[c, :, yh * 2 + yl, n] = block[:, yh, c, :, yl * 128 : yl * 128 + 128]

    def join(part, src):
        def step(i, carry):
            src[i] = (src[i].astype(F32) + part[core, i].astype(F32)).astype(BF)
            return carry

        lax.fori_loop(0, 4, step, 0)

    loads["gig"].wait()
    for n in range(4):
        put_table(eg["part"], n, mm(hot_own, gig[:, n * 256 : n * 256 + 256]))
    x_eg = swap(1, eg["part"].at[other], eg["src"])

    loads["pw"].wait()
    loads["emb"].wait()
    loads["slot"].wait()
    loads["gain"].wait()
    square = jnp.zeros((256, 1), F32)
    for n in range(4):
        at = slice(n * 256, n * 256 + 256)
        u_part = mm(slot[...], pw[:, at]) + mm_tn(hot[...], emb[:, at])
        norm[:, at] = u_part
        square = square + jnp.sum(u_part * u_part, axis=1, keepdims=True)
    scale_v = lax.rsqrt(square * (1.0 / 1024.0) + 1e-05)
    scale[...] = jnp.broadcast_to(scale_v, (256, 128))
    for n in range(4):
        at = slice(n * 256, n * 256 + 256)
        normed = norm[:, at] * scale_v
        norm[:, at] = normed
        r2[own, at] = (normed * gain[:, at]).astype(BF)
    x_r = swap(2, r2.at[own], r2.at[far])
    x_eg.wait_recv()
    join(eg["part"], eg["src"])
    glob.start(0)

    def t_swap(ref, base, j):
        rows = pl.ds(pl.multiple_of(j * 256, 256), 256)
        return remote(
            ref.at[other, rows, own], ref.at[other, rows, far], x_send.at[base + j], x_recv.at[base + j], partner
        )

    loads["up"].wait()

    def ff_step(j, carry):
        for k2 in range(2):
            k = j * 2 + k2
            at = pl.ds(pl.multiple_of(k * 256, 256), 256)
            rows = pl.ds(pl.multiple_of(k * 128, 128), 128)
            a = mm(r2[own, :], up[:, at])
            sig = jax.nn.sigmoid(a)
            h_t = (a * sig).astype(BF).T
            ht[0, rows, own] = h_t[:128]
            ht[1, rows, own] = h_t[128:]
            slope[k] = sig * (1.0 + a * (1.0 - sig))
        t_swap(ht, 6, j).start()
        return carry

    lax.fori_loop(0, 4, ff_step, 0)

    def da_step(j, carry):
        for k2 in range(2):
            k = j * 2 + k2
            at = pl.ds(pl.multiple_of(k * 256, 256), 256)
            rows = pl.ds(pl.multiple_of(k * 128, 128), 128)
            da_v = (mm_nt(og2[0].reshape(256, 1024), dn[at, :]) * slope[k]).astype(BF)
            da[:, at] = da_v
            da_t = da_v.T
            dat[0, rows, own] = da_t[:128]
            dat[1, rows, own] = da_t[128:]
        t_swap(dat, 10, j).start()
        return carry

    loads["dn"].wait()
    keep.wait()
    seven = pl.ds(0, 7)
    x_og = []
    for half in range(2):
        await_recv(og2.at[0, seven, half], ab_sem.at[1 + half], partner)
        x_og.append(swap((0, 4)[half], og2.at[0, :, half], og2.at[1, :, half]))
    lax.fori_loop(0, 2, da_step, 0)

    def units(src, table, first):
        return [
            Unit(src, t[:2], t[2], spot, device_at, unit_bufs[first + i], u_sem.at[first + i])
            for i, t in enumerate(table)
        ]

    d_units = units(dp, D_UNITS, 0)
    u_units = units(upart, U_UNITS, 3)
    p_units = units(pr, P_UNITS, 6)

    def big(lhs, rhs, out, n):
        at = slice(n * 256, n * 256 + 256)

        def step(g):
            rows = pl.ds(g * 512, 512)
            v = mm(lhs[core, rows, :], rhs(at)).astype(BF).reshape(2, 2, 4, 2, 16, 256)
            for xx in range(2):
                for yh in range(2):
                    for yl in range(2):
                        out[2 * g + xx, yh * 2 + yl, :, :, at] = v[xx, yh, :, yl]

        step(0)
        step(1)

    for j in range(4):
        t_swap(ht, 6, j).wait_recv()
    for copy in x_og:
        copy.wait_recv()

    def both_og(at):
        return og2[:, :, :, :, at].reshape(512, 256)

    def both_r(at):
        return r2[:, at]

    big(ht, both_og, dp, 0)
    d_units[0].one.start()
    big(ht, both_og, dp, 1)
    big(ht, both_og, dp, 2)
    d_units[1].one.start()
    big(ht, both_og, dp, 3)
    d_units[2].one.start()
    glob.finish(0)
    glob.start(1)
    lax.fori_loop(2, 4, da_step, 0)
    for n in range(4):
        at = slice(n * 256, n * 256 + 256)
        dr[:, at] = mm_nt(da[...], up[at, :])
    gain_v = gain[...]

    def du_step(i, total):
        rows = pl.ds(pl.multiple_of(i * 32, 32), 32)
        dr_v = dr[rows, :]
        normed = norm[rows, :]
        product = dr_v * normed
        dn_v = dr_v * gain_v
        mean = jnp.sum(product * gain_v, axis=1, keepdims=True) * (1.0 / 1024.0)
        du_v = og2[0, i].reshape(32, 1024).astype(F32) + scale[rows, 0:1] * (dn_v - normed * mean)
        du[rows, :] = du_v.astype(BF)
        return total + jnp.sum(product.reshape(4, 8, 1024), axis=0)

    gain_part = lax.fori_loop(0, 8, du_step, jnp.zeros((8, 1024), F32))
    for n in range(4):
        put_table(el["part"], n, mm(hot[...], du[:, n * 256 : n * 256 + 256]))
    x_el = swap(3, el["part"].at[other], el["src"])
    gp[0, core] = jnp.sum(gain_part, axis=0, keepdims=True)
    x_g = swap(5, gp.at[0, core], gp.at[0, core])
    for unit in d_units:
        unit.one.relay()
    x_el.wait_recv()
    join(el["part"], el["src"])
    loc.start(0)
    x_r.wait_recv()
    for j in range(4):
        t_swap(dat, 10, j).wait_recv()
    big(dat, both_r, upart, 0)
    u_units[0].one.start()
    big(dat, both_r, upart, 1)
    big(dat, both_r, upart, 2)
    u_units[1].one.start()
    big(dat, both_r, upart, 3)
    u_units[2].one.start()
    glob.finish(1)
    glob.start(2)
    for n in range(4):
        at = slice(n * 256, n * 256 + 256)
        dut[at, :] = du[:, at].T

    def gain_swap(step):
        axis = step - 1
        mine = gp.at[step, spot[axis]]
        for k in FAR_FIRST:
            device = device_at(axis, (spot[axis] + k) % 4)
            remote(mine, mine, g_sem.at[2 * axis], g_sem.at[2 * axis + 1], device).start()

    def gain_join(step):
        three = gp.at[step, pl.ds(0, 3)]
        await_recv(three, g_sem.at[2 * step - 1], partner)
        await_send(three, g_sem.at[2 * step - 2], partner)
        return gp[step, 0] + gp[step, 1] + gp[step, 2] + gp[step, 3]

    def p_swap(g):
        return remote(pp.at[other, g], pr.at[g], x_send.at[14 + g], x_recv.at[14 + g], partner)

    def proj_step(g, carry):
        rows = pl.ds(pl.multiple_of(g * 256, 256), 256)
        for n in range(2):
            lo, hi = slice(n * 256, n * 256 + 256), slice(512 + n * 256, 768 + n * 256)
            v_lo = mm(dut[rows, :], slot[:, lo]).reshape(2, 2, 4, 2, 8, 256)
            v_hi = mm(dut[rows, :], slot[:, hi]).reshape(2, 2, 4, 2, 8, 256)
            v = jnp.concatenate([v_lo, v_hi], axis=4).astype(BF)
            for c in range(2):
                for yh in range(2):
                    for yl in range(2):
                        pp[c, g, yh * 2 + yl, :, :, lo] = v[yh, c, :, yl]
        p_swap(g).start()
        return carry

    lax.fori_loop(0, 4, proj_step, 0)
    x_g.wait_recv()
    x_g.wait_send()
    gp[1, x] = gp[0, 0] + gp[0, 1]
    gain_swap(1)
    for n in range(4):
        at = slice(n * 256, n * 256 + 256)
        gog_o[:, at] = mm_nt(du[...], pw[at, :]).astype(BF)
    for g in range(4):
        p_swap(g).wait_recv()
    join(pp, pr)
    for unit in p_units:
        unit.one.start_far()
    loc.finish(0)
    loc.start(1)
    for unit in u_units:
        unit.one.relay()
    for unit in p_units:
        unit.one.start_near()
    for unit in d_units:
        unit.start2()
    for unit in p_units:
        unit.one.relay()
    loc.finish(1)
    loc.start(2)
    glob.finish(2)
    glob.start(3)
    for unit in u_units:
        unit.start2()
    gp[2, y] = gain_join(1)
    gain_swap(2)
    for unit in p_units:
        unit.start2()
    loc.finish(2)
    loc.start(3)
    for unit in d_units:
        unit.start3()
    for unit in u_units:
        unit.start3()
    gp[3, z] = gain_join(2)
    gain_swap(3)
    for unit in p_units:
        unit.start3()
    glob.finish(3)
    glob.start(4)
    for i, unit in enumerate(d_units):
        down_o[:, pl.ds(*D_UNITS[i][:2])] = unit.three.finish()
    gain_o[...] = gain_join(3)
    loc.finish(3)
    loc.start(4)
    for i, unit in enumerate(u_units):
        up_o[:, pl.ds(*U_UNITS[i][:2])] = unit.three.finish()
    for i, unit in enumerate(p_units):
        first, width, _ = P_UNITS[i]
        value = unit.three.finish()
        proj_o[:, pl.ds(first, width)] = value[:8]
        proj_o[:, pl.ds(512 + first, width)] = value[8:]
    glob.finish(4)
    glob.drain()
    for unit in d_units + u_units + p_units:
        unit.drain()
    for half in range(2):
        await_send(ogp.at[seven, half], ab_sem.at[0], partner)
    for copy in x_og + [x_eg, x_r, x_el]:
        copy.wait_send()
    for i in range(4):
        t_swap(ht, 6, i).wait_send()
        t_swap(dat, 10, i).wait_send()
        p_swap(i).wait_send()
    loc.finish(4)
    loc.drain()


def finish(gog, table_g, table_l, gain, proj, up, down, gog_o, embg_o, embl_o, gain_o, proj_o, up_o, down_o, embg, embl, sem):
    pairs = ((gog, gog_o), (gain, gain_o), (proj, proj_o), (up, up_o), (down, down_o))
    copies = [pltpu.make_async_copy(src, dst, sem.at[n]) for n, (src, dst) in enumerate(pairs)]
    for copy in copies:
        copy.start()
    for n, (table, value, out) in enumerate(((table_g, embg, embg_o), (table_l, embl, embl_o))):
        for row in range(16):
            px, yh, c = row // 4, row // 2 % 2, row % 2
            for col in range(8):
                pz, yl = col // 2, col % 2
                value[row * 16 : row * 16 + 16, col * 128 : col * 128 + 128] = table[c, px, yh * 2 + yl, pz].astype(F32)
        copy = pltpu.make_async_copy(value, out, sem.at[5 + n])
        copy.start()
        copies.append(copy)
    for copy in copies:
        copy.wait()


def on_device(
    byte_ids,
    global_out,
    global_in_grad,
    out_grad,
    proj_weight,
    emb_local,
    norm_gain,
    up_weight,
    down_weight,
):
    scratch = [pltpu.VMEM(shape, kind) for _, shape, kind in FIXED]
    scratch += [pltpu.VMEM(shape, BF) for _, shape in TABLE] * 2
    for _, width, order in ALL_UNITS:
        scratch += unit_scratch(width, order)
    dma = pltpu.SemaphoreType.DMA
    scratch += [dma((n,)) for n in (N_LOADS, N_X, N_X, 3, 6, 10, 10)] + [dma((len(ALL_UNITS), 7))]
    vmem = pl.BlockSpec(memory_space=pltpu.VMEM)
    anywhere = pl.BlockSpec(memory_space=pl.ANY)
    parts = pl.pallas_call(
        kernel,
        out_shape=(
            pltpu.VMEM((256, 1024), BF),
            pltpu.VMEM((2, 4, 4, 4, 16, 128), BF),
            pltpu.VMEM((2, 4, 4, 4, 16, 128), BF),
            pltpu.VMEM((1, 1024), F32),
            pltpu.VMEM((8, 1024), F32),
            pltpu.VMEM((16, 1024), F32),
            pltpu.VMEM((16, 1024), F32),
        ),
        in_specs=[pl.BlockSpec(memory_space=pltpu.HBM)] * 9,
        out_specs=[vmem] * 7,
        scratch_shapes=scratch,
        compiler_params=pltpu.CompilerParams(
            collective_id=0, has_side_effects=True, vmem_limit_bytes=52 * 1024 * 1024
        ),
    )(
        pltpu.with_memory_space_constraint(byte_ids.T, pltpu.HBM),
        global_out,
        global_in_grad,
        out_grad,
        proj_weight,
        emb_local,
        pltpu.with_memory_space_constraint(norm_gain.reshape(1, 1024), pltpu.HBM),
        up_weight,
        down_weight,
    )
    out = jax.ShapeDtypeStruct
    gog, embg, embl, gain, proj, up, down = pl.pallas_call(
        finish,
        out_shape=(
            out((256, 1024), BF),
            out((256, 1024), F32),
            out((256, 1024), F32),
            out((1, 1024), F32),
            out((8, 1024), F32),
            out((16, 1024), F32),
            out((16, 1024), F32),
        ),
        in_specs=[vmem] * 7,
        out_specs=[anywhere] * 7,
        scratch_shapes=[pltpu.VMEM((256, 1024), F32), pltpu.VMEM((256, 1024), F32), dma((7,))],
        compiler_params=pltpu.CompilerParams(vmem_limit_bytes=6 * 1024 * 1024),
    )(*parts)
    return gog, embg, embl, gain.reshape(1024), proj.T, up.T, down


def solution(mesh):
    placed = (
        P("seq", None),
        P("seq", "tp"),
        P("seq", "tp"),
        P(("seq", "tp"), None),
        P(),
        P(),
        P(),
        P(),
        P(),
    )
    return jax.shard_map(
        on_device,
        mesh=mesh,
        in_specs=placed,
        out_specs=(
            P("seq", "tp"),
            P(),
            P(),
            P(),
            P(None, ("seq", "tp")),
            P(None, ("seq", "tp")),
            P(("seq", "tp"), None),
        ),
        check_vma=False,
    )
```
